512 devices in a mesh: freq: 4 (over z_hi), layer: 8 (over x, z_lo), lat: 16 (over y, core).
Axes of the slice: x: 4, y: 8, z: 8 (z_hi: 4, z_lo: 2; z = z_hi * 2 + z_lo), core: 2. Of those that a mesh axis runs over, the one named last changes fastest.
Arguments:
- source: float32 [2, 4, 2, 8, 512, 512], P(None, 'freq', None, 'layer', 'lat'), may hold values from -6 to 6
- contrast: float32 [2, 4, 8, 512, 512], P(None, 'freq', 'layer', 'lat'), may hold values from -0.5 to 0.5
- green: float32 [2, 4, 8, 8, 512, 512], P(None, 'freq', None, 'layer', 'lat'), may hold values from -0.6 to 0.6
- efield: float32 [2, 4, 2, 8, 512, 512], P(None, 'freq', None, 'layer', 'lat'), may hold values from -6 to 6
- cell_class: int32 [8, 512, 512], P('layer', 'lat'), may hold values from 0 to 7
Outputs:
- cell_gradient: float32 [8, 512, 512], P('layer', 'lat')
- class_gradient: float32 [8, 8], P('layer')
The draws below stay inside these ranges and needn't reach their ends.
All inputs are finite; a program needn't handle non-finite values.
Results may differ from the reference program's by a relative error of at most 0.0001.
Values sent between devices are 32-bit elements; how exact they have to be, the bound alone decides.
A program may use at most 64 MiB of HBM per device.

```python
import jax
import jax.numpy as jnp
from jax import lax

NXY = 512
POLS = 2
ITERS = 2
CLASSES = 8
LAYERS = 8
FREQS = 4


def place_ends(entries, key, least, top_value):
    longest = entries.shape.index(max(entries.shape))
    spots = []
    for shift in (0, 1):
        where = [jax.random.randint(jax.random.fold_in(key, axis), (), 0, length) for axis, length in enumerate(entries.shape)]
        where[longest] = (where[longest] + shift) % entries.shape[longest]
        spots.append(tuple(where))
    return entries.at[spots[0]].set(least).at[spots[1]].set(top_value)


def steps_of(own_key, extent, pieces, smallest, top_value):
    gain = 1.0
    for dim, shards_of in pieces:
        steps = jax.random.uniform(jax.random.fold_in(jax.random.fold_in(own_key, 6), dim), (shards_of,), jnp.float32, smallest / len(pieces), top_value / len(pieces))
        gain = gain * jnp.repeat(jnp.exp(steps), extent[dim] // shards_of).reshape((-1,) + (1,) * (len(extent) - 1 - dim))
    return gain


def bell_draw(stream_key, shape, deviation, limit, shards=(), dtype=jnp.bfloat16):
    entries = jax.random.normal(stream_key, shape, jnp.float32) * deviation
    if len(shards) > 0:
        entries = steps_of(stream_key, shape, shards, -0.22, 0.18) * entries
    return jnp.clip(entries, min=-limit, max=limit).astype(dtype)


def setup_inputs(seed: int = 0) -> dict:
    splits = jax.random.split(jax.random.key(seed), 6)
    return {
        "source": bell_draw(splits[0], (2, FREQS, POLS, LAYERS, NXY, NXY), 1.0, 6.0, ((1, 4), (3, 8), (4, 16)), jnp.float32),
        "contrast": jnp.clip(jax.random.uniform(splits[1], (2, FREQS, LAYERS, NXY, NXY), jnp.float32, -0.5, 0.5) * steps_of(splits[1], (2, FREQS, LAYERS, NXY, NXY), ((1, 4), (2, 8), (3, 16)), -0.4, 0.0), -0.5, 0.5),
        "green": jnp.clip(jax.random.uniform(splits[2], (2, FREQS, LAYERS, LAYERS, NXY, NXY), jnp.float32, -0.6, 0.6) * steps_of(splits[2], (2, FREQS, LAYERS, LAYERS, NXY, NXY), ((1, 4), (3, 8), (4, 16)), -0.4, 0.0), -0.6, 0.6),
        "efield": bell_draw(splits[3], (2, FREQS, POLS, LAYERS, NXY, NXY), 1.0, 6.0, ((1, 4), (3, 8), (4, 16)), jnp.float32),
        "cell_class": place_ends(jax.random.randint(splits[4], (LAYERS, NXY, NXY), 0, CLASSES), jax.random.fold_in(splits[4], 1), 0, CLASSES - 1).astype(jnp.int32),
    }


def one_frequency(items):
    src, con, grn, fwd = items
    start = src[0] + 1j * src[1]
    factor = (con[0] + 1j * con[1])[None]
    kernel = grn[0] + 1j * grn[1]
    field = start
    for step in range(ITERS):
        weighted = factor * field
        spectra = jnp.swapaxes(jnp.fft.fft2(weighted, norm="ortho"), -1, -2)
        mixed = jnp.einsum("oiyx,piyx->poyx", kernel, spectra)
        back = jnp.fft.ifft2(jnp.swapaxes(mixed, -1, -2), norm="ortho")
        field = start + factor * back
    return jnp.sum(fwd[0] * jnp.real(field) - fwd[1] * jnp.imag(field), axis=0)


def reference(source, contrast, green, efield, cell_class):
    per_freq = lax.map(one_frequency, (jnp.moveaxis(source, 1, 0), jnp.moveaxis(contrast, 1, 0), jnp.moveaxis(green, 1, 0), jnp.moveaxis(efield, 1, 0)))
    cell = jnp.sum(per_freq, axis=0).astype(jnp.float32)
    sums = [jnp.sum(jnp.where(cell_class == c, cell, jnp.zeros_like(cell)), axis=(1, 2)) for c in range(CLASSES)]
    classes = (jnp.stack(sums, axis=1) / float(NXY)).astype(jnp.float32)
    return cell, classes
```

```python
import functools

import jax
import jax.numpy as jnp
import numpy as np
from jax import lax
from jax.experimental import pallas as pl
from jax.experimental.pallas import tpu as pltpu
from jax.sharding import PartitionSpec as P

ITERS = 2
CLASSES = 8
LANES = 128
MESH = pl.DeviceIdType.MESH
F32 = jnp.float32
BF16 = jnp.bfloat16


def tables(length):
    index = np.arange(length)
    angle = (index[:, None] * index[None, :] % length) * (2.0 * np.pi / length)
    both = np.concatenate([np.cos(angle), np.sin(angle)]) / np.sqrt(length)
    high = both.astype(BF16)
    low = (both - high.astype(np.float64)).astype(BF16)
    return high, low


def split(value):
    high = value.astype(BF16)
    return high, (value - high.astype(F32)).astype(BF16)


def dot(a, b):
    return jnp.dot(a, b, preferred_element_type=F32)


def lane_of(shape):
    return lax.broadcasted_iota(jnp.int32, shape, len(shape) - 1)


def turn_lanes(parts):
    lane = lane_of(parts[0].shape)
    odd = (lane // 32) % 2 == 1
    low = lane < 64
    pairs = []
    for first, second in ((parts[0], parts[1]), (parts[2], parts[3])):
        pairs.append(
            (
                jnp.where(odd, pltpu.roll(second, 32, 1), first),
                jnp.where(odd, second, pltpu.roll(first, LANES - 32, 1)),
            )
        )
    (t0, t1), (t2, t3) = pairs
    return (
        jnp.where(low, t0, pltpu.roll(t2, 64, 1)),
        jnp.where(low, t1, pltpu.roll(t3, 64, 1)),
        jnp.where(low, pltpu.roll(t0, 64, 1), t2),
        jnp.where(low, pltpu.roll(t1, 64, 1), t3),
    )


def turned(value, sign):
    real = (lane_of(value.shape) // 32) % 2 == 0
    return jnp.where(real, -sign * pltpu.roll(value, LANES - 32, 1), sign * pltpu.roll(value, 32, 1))


def kernel(
    lat, layers, freqs, n,
    src_hbm, con_hbm, grn_hbm, efd_hbm, cls_hbm, high_hbm, low_hbm,
    cell_out, class_out,
    src, con, grn, efd, cls, high, low,
    field, rows_buf, cols_buf, prod,
    send_a, recv_a, send_b, recv_b, send_c, recv_c, send_d, recv_d,
    send_g, recv_g, wide_g,
    terms, recv_t, cell, part, recv_l, part_f, recv_k,
    load_sem, own_sem,
    sa_sem, ra_sem, sb_sem, rb_sem, sc_sem, rc_sem, sd_sem, rd_sem,
    sg_sem, rg_sem, st_sem, rt_sem, sl_sem, rl_sem, su_sem, ru_sem, sk_sem, rk_sem,
):
    at = {"lat": lax.axis_index("lat"), "layer": lax.axis_index("layer"), "freq": lax.axis_index("freq")}
    size = {"lat": lat, "layer": layers, "freq": freqs}
    wide = n // layers
    groups = 2 * layers // 4

    barrier = pltpu.get_barrier_semaphore()
    for axis in ("lat", "layer", "freq"):
        def greet(k, carry, axis=axis):
            peer = lax.rem(at[axis] + k, size[axis])
            pl.semaphore_signal(barrier, inc=1, device_id={axis: peer}, device_id_type=MESH)
            return carry
        lax.fori_loop(1, size[axis], greet, 0)

    loads = [
        pltpu.make_async_copy(a, b, load_sem.at[i])
        for i, (a, b) in enumerate(
            ((src_hbm, src), (con_hbm, con), (high_hbm, high), (low_hbm, low), (grn_hbm, grn), (efd_hbm, efd), (cls_hbm, cls))
        )
    ]
    for load in loads:
        load.start()

    def remote(axis, peer, source, target, send_sem, recv_sem):
        return pltpu.make_async_remote_copy(
            src_ref=source, dst_ref=target, send_sem=send_sem, recv_sem=recv_sem,
            device_id={axis: peer}, device_id_type=MESH,
        )

    def each_peer(axis, act):
        def one(k, carry):
            act(lax.rem(at[axis] + k, size[axis]))
            return carry
        lax.fori_loop(1, size[axis], one, 0)

    def swap(axis, source, target, rows, send_sem, recv_sem, own):
        me = at[axis]
        def block(ref, i):
            return ref.at[pl.ds(pl.multiple_of(i * rows, 8), rows)]
        def copy(peer, landing):
            return remote(axis, peer, block(source, peer), block(target, landing), send_sem.at[peer], recv_sem.at[landing])
        def mine():
            return pltpu.make_async_copy(block(source, me), block(target, me), own)
        def start():
            each_peer(axis, lambda peer: copy(peer, me).start())
            mine().start()
        def arrived():
            each_peer(axis, lambda peer: copy(peer, peer).wait_recv())
            mine().wait()
        def sent():
            each_peer(axis, lambda peer: copy(peer, me).wait_send())
        return start, arrived, sent

    def spread(axis, source, target, send_sem, recv_sem, own):
        me = at[axis]
        def copy(peer, landing):
            return remote(axis, peer, source, target.at[landing], send_sem.at[peer], recv_sem.at[landing])
        def mine():
            return pltpu.make_async_copy(source, target.at[me], own)
        def start():
            each_peer(axis, lambda peer: copy(peer, me).start())
            mine().start()
        def arrived():
            each_peer(axis, lambda peer: copy(peer, peer).wait_recv())
            mine().wait()
        def sent():
            each_peer(axis, lambda peer: copy(peer, me).wait_send())
        return start, arrived, sent

    green_copies = swap("layer", send_g, recv_g, groups * wide, sg_sem, rg_sem, own_sem.at[8])

    def exchanges(step):
        return (
            swap("lat", send_a.at[step], recv_a.at[step], 32, sa_sem.at[step], ra_sem.at[step], own_sem.at[step * 4]),
            swap("layer", send_b.at[step], recv_b.at[step], wide, sb_sem.at[step], rb_sem.at[step], own_sem.at[step * 4 + 1]),
            swap("layer", send_c.at[step], recv_c.at[step], wide, sc_sem.at[step], rc_sem.at[step], own_sem.at[step * 4 + 2]),
            swap("lat", send_d.at[step], recv_d.at[step], 32, sd_sem.at[step], rd_sem.at[step], own_sem.at[step * 4 + 3]),
        )

    chunk = min(256, n)

    def lane_transform(start, width):
        whole = rows_buf[...]
        upper = rows_buf[0:LANES]
        out = []
        for base in (0, n):
            product = dot(whole, high[base:base + n, start:start + width])
            out.append(product[:LANES] + product[LANES:] + dot(upper, low[base:base + n, start:start + width]))
        return out

    def row_transform(source, target, sign):
        upper, lower = split(source[...])
        cols_buf[:, 0:LANES] = upper
        cols_buf[:, LANES:2 * LANES] = lower
        prod[...] = dot(high[...], cols_buf[...])
        tail = dot(low[...], cols_buf[:, 0:LANES])
        full = prod[:, 0:LANES] + prod[:, LANES:2 * LANES] + tail
        target[...] = full[:n] + turned(full[n:], sign)

    loads[0].wait()
    loads[1].wait()
    field[...] = src[...]
    loads[2].wait()
    loads[3].wait()

    def iterate(step, carry):
        (start_a, came_a, _), (start_b, came_b, _), (start_c, came_c, _), (start_d, came_d, _) = exchanges(step)

        for pol in range(2):
            for piece, value in enumerate(
                (
                    con[0] * field[0, pol] - con[1] * field[1, pol],
                    con[0] * field[1, pol] + con[1] * field[0, pol],
                )
            ):
                row = piece * 64 + pol * 32
                upper, lower = split(value)
                rows_buf[row:row + 32] = upper
                rows_buf[LANES + row:LANES + row + 32] = lower
        for start in range(0, n, chunk):
            cosine, sine = lane_transform(start, chunk)
            real = cosine[:64] + sine[64:]
            imag = cosine[64:] - sine[:64]
            for tile in range(chunk // LANES):
                lanes = slice(tile * LANES, (tile + 1) * LANES)
                blocks = turn_lanes((real[:32, lanes], imag[:32, lanes], real[32:, lanes], imag[32:, lanes]))
                for g, block in enumerate(blocks):
                    row = (start // LANES + tile) * LANES + g * 32
                    send_a[step, row:row + 32] = block

        @pl.when(step == 0)
        def _():
            pl.semaphore_wait(barrier, lat + layers + freqs - 3)

        start_a()

        @pl.when(step == 0)
        def _():
            loads[4].wait()
            for g in range(groups):
                for tile in range(n // LANES):
                    rows = grn[4 * g:4 * g + 4, :, tile * LANES:(tile + 1) * LANES].reshape(LANES, LANES)
                    flipped = rows.T
                    for half in range(LANES // wide):
                        row = ((tile * LANES // wide + half) * groups + g) * wide
                        send_g[row:row + wide] = flipped[half * wide:(half + 1) * wide]
            green_copies[0]()

        came_a()
        row_transform(recv_a.at[step], send_b.at[step], -1.0)
        start_b()

        @pl.when(step == 0)
        def _():
            green_copies[1]()
            def widen(i, carry):
                value = recv_g[pl.ds(pl.multiple_of(i * wide, 8), wide)]
                lane = lane_of(value.shape)
                low_half = lane < 64
                odd = (lane // 32) % 2 == 1
                moved = pltpu.roll(value, 64, 1)
                for pair, double in enumerate((jnp.where(low_half, value, moved), jnp.where(low_half, moved, value))):
                    other = pltpu.roll(double, 32, 1)
                    wide_g[i * 4 + pair * 2] = jnp.where(odd, other, double)
                    wide_g[i * 4 + pair * 2 + 1] = jnp.where(odd, double, other)
                return carry
            lax.fori_loop(0, layers * groups, widen, 0)

        came_b()

        def mix(r, carry):
            base = pl.multiple_of(r * 8, 8)
            sums = [None] * layers
            for l in range(layers):
                value = recv_b[step, pl.ds(pl.multiple_of(l * wide + base, 8), 8)]
                side = turned(value, 1.0)
                for o in range(layers):
                    term = (
                        wide_g[l * 2 * layers + o, pl.ds(base, 8)] * value
                        + wide_g[l * 2 * layers + layers + o, pl.ds(base, 8)] * side
                    )
                    sums[o] = term if l == 0 else sums[o] + term
            for o in range(layers):
                send_c[step, pl.ds(pl.multiple_of(o * wide + base, 8), 8)] = sums[o]
            return carry

        lax.fori_loop(0, wide // 8, mix, 0)
        start_c()
        came_c()
        row_transform(recv_c.at[step], send_d.at[step], 1.0)
        start_d()
        came_d()

        for tile in range(n // LANES):
            blocks = turn_lanes([recv_d[step, tile * LANES + g * 32:tile * LANES + g * 32 + 32] for g in range(4)])
            for q, block in enumerate(blocks):
                pol, piece = q // 2, q % 2
                row = piece * 64 + pol * 32
                upper, lower = split(block)
                rows_buf[row:row + 32, tile * LANES:(tile + 1) * LANES] = upper
                rows_buf[LANES + row:LANES + row + 32, tile * LANES:(tile + 1) * LANES] = lower
        for start in range(0, n, chunk):
            lanes = slice(start, start + chunk)
            cosine, sine = lane_transform(start, chunk)
            real = cosine[:64] - sine[64:]
            imag = cosine[64:] + sine[:64]
            for pol in range(2):
                rows = slice(pol * 32, pol * 32 + 32)
                field[0, pol, :, lanes] = src[0, pol, :, lanes] + con[0, :, lanes] * real[rows] - con[1, :, lanes] * imag[rows]
                field[1, pol, :, lanes] = src[1, pol, :, lanes] + con[0, :, lanes] * imag[rows] + con[1, :, lanes] * real[rows]
        return carry

    lax.fori_loop(0, ITERS, iterate, 0)

    loads[5].wait()
    loads[6].wait()
    total = efd[0, 0] * field[0, 0] - efd[1, 0] * field[1, 0]
    total = total + (efd[0, 1] * field[0, 1] - efd[1, 1] * field[1, 1])
    terms[...] = total
    own_rows = 32 // freqs
    scatter = swap("freq", terms, recv_t, own_rows, st_sem, rt_sem, own_sem.at[9])
    scatter[0]()

    for c in range(CLASSES):
        line = jnp.sum(jnp.where(cls[...] == c, total, 0.0), axis=0, keepdims=True)
        line = sum(line[:, t * LANES:(t + 1) * LANES] for t in range(n // LANES))
        part[c:c + 1] = line
    lat_sums = spread("lat", part, recv_l, sl_sem, rl_sem, own_sem.at[10])
    lat_sums[0]()

    scatter[1]()
    mine = recv_t[0:own_rows]
    for f in range(1, freqs):
        mine = mine + recv_t[f * own_rows:(f + 1) * own_rows]
    own = pl.ds(pl.multiple_of(at["freq"] * own_rows, 8), own_rows)
    cell[own] = mine

    def gather(peer, landing):
        rows = pl.ds(pl.multiple_of(landing * own_rows, 8), own_rows)
        return remote("freq", peer, cell.at[rows], cell.at[rows], su_sem.at[peer], ru_sem.at[landing])

    each_peer("freq", lambda peer: gather(peer, at["freq"]).start())

    lat_sums[1]()
    part_f[...] = jnp.sum(recv_l[...], axis=0)
    freq_sums = spread("freq", part_f, recv_k, sk_sem, rk_sem, own_sem.at[11])
    freq_sums[0]()

    each_peer("freq", lambda peer: gather(peer, peer).wait_recv())
    cell_out[...] = cell[...]
    freq_sums[1]()
    sums = jnp.sum(jnp.sum(recv_k[...], axis=0), axis=1, keepdims=True) / float(n)
    spot = lax.broadcasted_iota(jnp.int32, (CLASSES, LANES), 0) == lane_of((CLASSES, LANES))
    class_out[...] = jnp.sum(jnp.where(spot, sums, 0.0), axis=0, keepdims=True)[:, :CLASSES]

    def drain(step, carry):
        for exchange in exchanges(step):
            exchange[2]()
        return carry

    lax.fori_loop(0, ITERS, drain, 0)
    green_copies[2]()
    scatter[2]()
    lat_sums[2]()
    each_peer("freq", lambda peer: gather(peer, at["freq"]).wait_send())
    freq_sums[2]()


def per_device(lat, layers, freqs, source, contrast, green, efield, cell_class):
    n = source.shape[5]
    high, low = tables(n)
    wide = n // layers
    own_rows = 32 // freqs
    dma = pltpu.SemaphoreType.DMA
    stage = pltpu.VMEM((ITERS, n, LANES), F32)
    scratch = [
        pltpu.VMEM((2, 2, 32, n), F32),
        pltpu.VMEM((2, 32, n), F32),
        pltpu.VMEM((2 * layers, 32, n), F32),
        pltpu.VMEM((2, 2, 32, n), F32),
        pltpu.VMEM((32, n), jnp.int32),
        pltpu.VMEM((2 * n, n), BF16),
        pltpu.VMEM((2 * n, n), BF16),
        pltpu.VMEM((2, 2, 32, n), F32),
        pltpu.VMEM((2 * LANES, n), BF16),
        pltpu.VMEM((n, 2 * LANES), BF16),
        pltpu.VMEM((2 * n, 2 * LANES), F32),
        *[stage] * 8,
        pltpu.VMEM((layers * n // 2, LANES), F32),
        pltpu.VMEM((layers * n // 2, LANES), F32),
        pltpu.VMEM((layers * 2 * layers, wide, LANES), F32),
        pltpu.VMEM((32, n), F32),
        pltpu.VMEM((32, n), F32),
        pltpu.VMEM((32, n), F32),
        pltpu.VMEM((CLASSES, LANES), F32),
        pltpu.VMEM((lat, CLASSES, LANES), F32),
        pltpu.VMEM((CLASSES, LANES), F32),
        pltpu.VMEM((freqs, CLASSES, LANES), F32),
        dma((7,)),
        dma((12,)),
        *[dma((ITERS, lat))] * 2,
        *[dma((ITERS, layers))] * 4,
        *[dma((ITERS, lat))] * 2,
        *[dma((layers,))] * 2,
        *[dma((freqs,))] * 2,
        *[dma((lat,))] * 2,
        *[dma((freqs,))] * 4,
    ]
    cell, classes = pl.pallas_call(
        functools.partial(kernel, lat, layers, freqs, n),
        out_shape=(jax.ShapeDtypeStruct((32, n), F32), jax.ShapeDtypeStruct((1, CLASSES), F32)),
        in_specs=[pl.BlockSpec(memory_space=pl.ANY)] * 7,
        out_specs=(pl.BlockSpec(memory_space=pltpu.VMEM), pl.BlockSpec(memory_space=pltpu.VMEM)),
        scratch_shapes=scratch,
        compiler_params=pltpu.CompilerParams(
            collective_id=0, has_side_effects=True, vmem_limit_bytes=48 * 1024 * 1024
        ),
    )(
        source.reshape(2, 2, 32, n),
        contrast.reshape(2, 32, n),
        green.reshape(2 * layers, 32, n),
        efield.reshape(2, 2, 32, n),
        cell_class.reshape(32, n),
        jnp.asarray(high),
        jnp.asarray(low),
    )
    return cell.reshape(1, 32, n), classes


def solution(mesh):
    placed = (
        P(None, "freq", None, "layer", "lat", None),
        P(None, "freq", "layer", "lat", None),
        P(None, "freq", None, "layer", "lat", None),
        P(None, "freq", None, "layer", "lat", None),
        P("layer", "lat", None),
    )
    sizes = (mesh.shape["lat"], mesh.shape["layer"], mesh.shape["freq"])
    return jax.shard_map(
        functools.partial(per_device, *sizes),
        mesh=mesh,
        in_specs=placed,
        out_specs=(P("layer", "lat", None), P("layer", None)),
        check_vma=False,
    )
```

```python
import functools

import jax
import jax.numpy as jnp
import numpy as np
from jax import lax
from jax.experimental import pallas as pl
from jax.experimental.pallas import tpu as pltpu
from jax.sharding import PartitionSpec as P

ITERS = 2
CLASSES = 8
LANES = 128
MESH = pl.DeviceIdType.MESH
F32 = jnp.float32
BF16 = jnp.bfloat16


def tables(length):
    index = np.arange(length)
    angle = (index[:, None] * index[None, :] % length) * (2.0 * np.pi / length)
    both = np.concatenate([np.cos(angle), np.sin(angle)]) / np.sqrt(length)
    high = both.astype(BF16)
    low = (both - high.astype(np.float64)).astype(BF16)
    return high, low


def split(value):
    high = value.astype(BF16)
    return high, (value - high.astype(F32)).astype(BF16)


def dot(a, b):
    return jnp.dot(a, b, preferred_element_type=F32)


def lane_of(shape):
    return lax.broadcasted_iota(jnp.int32, shape, len(shape) - 1)


def turn_lanes(parts):
    lane = lane_of(parts[0].shape)
    odd = (lane // 32) % 2 == 1
    low = lane < 64
    pairs = []
    for first, second in ((parts[0], parts[1]), (parts[2], parts[3])):
        pairs.append(
            (
                jnp.where(odd, pltpu.roll(second, 32, 1), first),
                jnp.where(odd, second, pltpu.roll(first, LANES - 32, 1)),
            )
        )
    (t0, t1), (t2, t3) = pairs
    return (
        jnp.where(low, t0, pltpu.roll(t2, 64, 1)),
        jnp.where(low, t1, pltpu.roll(t3, 64, 1)),
        jnp.where(low, pltpu.roll(t0, 64, 1), t2),
        jnp.where(low, pltpu.roll(t1, 64, 1), t3),
    )


def turned(value, sign):
    real = (lane_of(value.shape) // 32) % 2 == 0
    return jnp.where(real, -sign * pltpu.roll(value, LANES - 32, 1), sign * pltpu.roll(value, 32, 1))


def kernel(
    lat, layers, freqs, n,
    src_hbm, con_hbm, grn_hbm, efd_hbm, cls_hbm, high_hbm, low_hbm,
    cell_out, class_out,
    src, con, grn, efd, cls, high, low,
    field, rows_buf, cols_buf, prod,
    send_a, recv_a, send_b, recv_b, send_c, recv_c, send_d, recv_d,
    send_g, recv_g, wide_g,
    terms, recv_t, cell, part, recv_l, part_f, recv_k,
    load_sem, own_sem,
    sa_sem, ra_sem, sb_sem, rb_sem, sc_sem, rc_sem, sd_sem, rd_sem,
    sg_sem, rg_sem, st_sem, rt_sem, sl_sem, rl_sem, su_sem, ru_sem, sk_sem, rk_sem,
):
    at = {"lat": lax.axis_index("lat"), "layer": lax.axis_index("layer"), "freq": lax.axis_index("freq")}
    size = {"lat": lat, "layer": layers, "freq": freqs}
    wide = n // layers
    groups = 2 * layers // 4

    barrier = pltpu.get_barrier_semaphore()
    for axis in ("lat", "layer", "freq"):
        def greet(k, carry, axis=axis):
            peer = lax.rem(at[axis] + k, size[axis])
            pl.semaphore_signal(barrier, inc=1, device_id={axis: peer}, device_id_type=MESH)
            return carry
        lax.fori_loop(1, size[axis], greet, 0)

    loads = [
        pltpu.make_async_copy(a, b, load_sem.at[i])
        for i, (a, b) in enumerate(
            ((src_hbm, src), (con_hbm, con), (high_hbm, high), (low_hbm, low), (grn_hbm, grn), (efd_hbm, efd), (cls_hbm, cls))
        )
    ]
    for load in loads:
        load.start()

    def remote(axis, peer, source, target, send_sem, recv_sem):
        return pltpu.make_async_remote_copy(
            src_ref=source, dst_ref=target, send_sem=send_sem, recv_sem=recv_sem,
            device_id={axis: peer}, device_id_type=MESH,
        )

    def each_peer(axis, act):
        pair = 1 if axis == "freq" else 2
        ring = size[axis] // pair
        def one(k, carry):
            i = k // pair
            ahead = i % 2
            hop = ahead * (ring // 2 - (i + 1) // 2) + (1 - ahead) * (ring - ring // 2 + i // 2)
            place = lax.rem(at[axis] // pair + hop, ring)
            act(place * pair + (at[axis] + pair - 1 - k % pair) % pair)
            return carry
        lax.fori_loop(0, size[axis] - 1, one, 0)

    def swap(axis, source, target, rows, send_sem, recv_sem, own):
        me = at[axis]
        def block(ref, i):
            return ref.at[pl.ds(pl.multiple_of(i * rows, 8), rows)]
        def copy(peer, landing):
            return remote(axis, peer, block(source, peer), block(target, landing), send_sem.at[peer], recv_sem.at[landing])
        def mine():
            return pltpu.make_async_copy(block(source, me), block(target, me), own)
        def start():
            each_peer(axis, lambda peer: copy(peer, me).start())
            mine().start()
        def arrived():
            each_peer(axis, lambda peer: copy(peer, peer).wait_recv())
            mine().wait()
        def sent():
            each_peer(axis, lambda peer: copy(peer, me).wait_send())
        return start, arrived, sent

    def spread(axis, source, target, send_sem, recv_sem, own):
        me = at[axis]
        def copy(peer, landing):
            return remote(axis, peer, source, target.at[landing], send_sem.at[peer], recv_sem.at[landing])
        def mine():
            return pltpu.make_async_copy(source, target.at[me], own)
        def start():
            each_peer(axis, lambda peer: copy(peer, me).start())
            mine().start()
        def arrived():
            each_peer(axis, lambda peer: copy(peer, peer).wait_recv())
            mine().wait()
        def sent():
            each_peer(axis, lambda peer: copy(peer, me).wait_send())
        return start, arrived, sent

    green_copies = swap("layer", send_g, recv_g, groups * wide, sg_sem, rg_sem, own_sem.at[8])

    def exchanges(step):
        return (
            swap("lat", send_a.at[step], recv_a.at[step], 32, sa_sem.at[step], ra_sem.at[step], own_sem.at[step * 4]),
            swap("layer", send_b.at[step], recv_b.at[step], wide, sb_sem.at[step], rb_sem.at[step], own_sem.at[step * 4 + 1]),
            swap("layer", send_c.at[step], recv_c.at[step], wide, sc_sem.at[step], rc_sem.at[step], own_sem.at[step * 4 + 2]),
            swap("lat", send_d.at[step], recv_d.at[step], 32, sd_sem.at[step], rd_sem.at[step], own_sem.at[step * 4 + 3]),
        )

    chunk = min(256, n)

    def lane_transform(start, width):
        whole = rows_buf[...]
        upper = rows_buf[0:LANES]
        out = []
        for base in (0, n):
            product = dot(whole, high[base:base + n, start:start + width])
            out.append(product[:LANES] + product[LANES:] + dot(upper, low[base:base + n, start:start + width]))
        return out

    def row_transform(source, target, sign):
        upper, lower = split(source[...])
        cols_buf[:, 0:LANES] = upper
        cols_buf[:, LANES:2 * LANES] = lower
        prod[...] = dot(high[...], cols_buf[...])
        tail = dot(low[...], cols_buf[:, 0:LANES])
        full = prod[:, 0:LANES] + prod[:, LANES:2 * LANES] + tail
        target[...] = full[:n] + turned(full[n:], sign)

    loads[0].wait()
    loads[1].wait()
    field[...] = src[...]
    loads[2].wait()
    loads[3].wait()

    def iterate(step, carry):
        (start_a, came_a, _), (start_b, came_b, _), (start_c, came_c, _), (start_d, came_d, _) = exchanges(step)

        for pol in range(2):
            for piece, value in enumerate(
                (
                    con[0] * field[0, pol] - con[1] * field[1, pol],
                    con[0] * field[1, pol] + con[1] * field[0, pol],
                )
            ):
                row = piece * 64 + pol * 32
                upper, lower = split(value)
                rows_buf[row:row + 32] = upper
                rows_buf[LANES + row:LANES + row + 32] = lower
        for start in range(0, n, chunk):
            cosine, sine = lane_transform(start, chunk)
            real = cosine[:64] + sine[64:]
            imag = cosine[64:] - sine[:64]
            for tile in range(chunk // LANES):
                lanes = slice(tile * LANES, (tile + 1) * LANES)
                blocks = turn_lanes((real[:32, lanes], imag[:32, lanes], real[32:, lanes], imag[32:, lanes]))
                for g, block in enumerate(blocks):
                    row = (start // LANES + tile) * LANES + g * 32
                    send_a[step, row:row + 32] = block

        @pl.when(step == 0)
        def _():
            loads[4].wait()
            for g in range(groups):
                for tile in range(n // LANES):
                    rows = grn[4 * g:4 * g + 4, :, tile * LANES:(tile + 1) * LANES].reshape(LANES, LANES)
                    flipped = rows.T
                    for half in range(LANES // wide):
                        row = ((tile * LANES // wide + half) * groups + g) * wide
                        send_g[row:row + wide] = flipped[half * wide:(half + 1) * wide]
            pl.semaphore_wait(barrier, lat + layers + freqs - 3)

        start_a()

        @pl.when(step == 0)
        def _():
            green_copies[0]()

        came_a()
        row_transform(recv_a.at[step], send_b.at[step], -1.0)
        start_b()

        @pl.when(step == 0)
        def _():
            green_copies[1]()
            def widen(i, carry):
                value = recv_g[pl.ds(pl.multiple_of(i * wide, 8), wide)]
                lane = lane_of(value.shape)
                low_half = lane < 64
                odd = (lane // 32) % 2 == 1
                moved = pltpu.roll(value, 64, 1)
                for pair, double in enumerate((jnp.where(low_half, value, moved), jnp.where(low_half, moved, value))):
                    other = pltpu.roll(double, 32, 1)
                    wide_g[i * 4 + pair * 2] = jnp.where(odd, other, double)
                    wide_g[i * 4 + pair * 2 + 1] = jnp.where(odd, double, other)
                return carry
            lax.fori_loop(0, layers * groups, widen, 0)

        came_b()

        def mix(r, carry):
            base = pl.multiple_of(r * 8, 8)
            sums = [None] * layers
            for l in range(layers):
                value = recv_b[step, pl.ds(pl.multiple_of(l * wide + base, 8), 8)]
                side = turned(value, 1.0)
                for o in range(layers):
                    term = (
                        wide_g[l * 2 * layers + o, pl.ds(base, 8)] * value
                        + wide_g[l * 2 * layers + layers + o, pl.ds(base, 8)] * side
                    )
                    sums[o] = term if l == 0 else sums[o] + term
            for o in range(layers):
                send_c[step, pl.ds(pl.multiple_of(o * wide + base, 8), 8)] = sums[o]
            return carry

        lax.fori_loop(0, wide // 8, mix, 0)
        start_c()
        came_c()
        row_transform(recv_c.at[step], send_d.at[step], 1.0)
        start_d()
        came_d()

        for tile in range(n // LANES):
            blocks = turn_lanes([recv_d[step, tile * LANES + g * 32:tile * LANES + g * 32 + 32] for g in range(4)])
            for q, block in enumerate(blocks):
                pol, piece = q // 2, q % 2
                row = piece * 64 + pol * 32
                upper, lower = split(block)
                rows_buf[row:row + 32, tile * LANES:(tile + 1) * LANES] = upper
                rows_buf[LANES + row:LANES + row + 32, tile * LANES:(tile + 1) * LANES] = lower
        for start in range(0, n, chunk):
            lanes = slice(start, start + chunk)
            cosine, sine = lane_transform(start, chunk)
            real = cosine[:64] - sine[64:]
            imag = cosine[64:] + sine[:64]
            for pol in range(2):
                rows = slice(pol * 32, pol * 32 + 32)
                field[0, pol, :, lanes] = src[0, pol, :, lanes] + con[0, :, lanes] * real[rows] - con[1, :, lanes] * imag[rows]
                field[1, pol, :, lanes] = src[1, pol, :, lanes] + con[0, :, lanes] * imag[rows] + con[1, :, lanes] * real[rows]
        return carry

    lax.fori_loop(0, ITERS, iterate, 0)

    loads[5].wait()
    loads[6].wait()
    total = efd[0, 0] * field[0, 0] - efd[1, 0] * field[1, 0]
    total = total + (efd[0, 1] * field[0, 1] - efd[1, 1] * field[1, 1])
    terms[...] = total
    own_rows = 32 // freqs
    scatter = swap("freq", terms, recv_t, own_rows, st_sem, rt_sem, own_sem.at[9])
    scatter[0]()

    for c in range(CLASSES):
        line = jnp.sum(jnp.where(cls[...] == c, total, 0.0), axis=0, keepdims=True)
        line = sum(line[:, t * LANES:(t + 1) * LANES] for t in range(n // LANES))
        part[c:c + 1] = line
    lat_sums = spread("lat", part, recv_l, sl_sem, rl_sem, own_sem.at[10])
    lat_sums[0]()

    scatter[1]()
    mine = recv_t[0:own_rows]
    for f in range(1, freqs):
        mine = mine + recv_t[f * own_rows:(f + 1) * own_rows]
    own = pl.ds(pl.multiple_of(at["freq"] * own_rows, 8), own_rows)
    cell[own] = mine

    def gather(peer, landing):
        rows = pl.ds(pl.multiple_of(landing * own_rows, 8), own_rows)
        return remote("freq", peer, cell.at[rows], cell.at[rows], su_sem.at[peer], ru_sem.at[landing])

    each_peer("freq", lambda peer: gather(peer, at["freq"]).start())

    lat_sums[1]()
    part_f[...] = jnp.sum(recv_l[...], axis=0)
    freq_sums = spread("freq", part_f, recv_k, sk_sem, rk_sem, own_sem.at[11])
    freq_sums[0]()

    each_peer("freq", lambda peer: gather(peer, peer).wait_recv())
    cell_out[...] = cell[...]
    freq_sums[1]()
    sums = jnp.sum(jnp.sum(recv_k[...], axis=0), axis=1, keepdims=True) / float(n)
    spot = lax.broadcasted_iota(jnp.int32, (CLASSES, LANES), 0) == lane_of((CLASSES, LANES))
    class_out[...] = jnp.sum(jnp.where(spot, sums, 0.0), axis=0, keepdims=True)[:, :CLASSES]

    def drain(step, carry):
        for exchange in exchanges(step):
            exchange[2]()
        return carry

    lax.fori_loop(0, ITERS, drain, 0)
    green_copies[2]()
    scatter[2]()
    lat_sums[2]()
    each_peer("freq", lambda peer: gather(peer, at["freq"]).wait_send())
    freq_sums[2]()


def per_device(lat, layers, freqs, source, contrast, green, efield, cell_class):
    n = source.shape[5]
    high, low = tables(n)
    wide = n // layers
    own_rows = 32 // freqs
    dma = pltpu.SemaphoreType.DMA
    stage = pltpu.VMEM((ITERS, n, LANES), F32)
    scratch = [
        pltpu.VMEM((2, 2, 32, n), F32),
        pltpu.VMEM((2, 32, n), F32),
        pltpu.VMEM((2 * layers, 32, n), F32),
        pltpu.VMEM((2, 2, 32, n), F32),
        pltpu.VMEM((32, n), jnp.int32),
        pltpu.VMEM((2 * n, n), BF16),
        pltpu.VMEM((2 * n, n), BF16),
        pltpu.VMEM((2, 2, 32, n), F32),
        pltpu.VMEM((2 * LANES, n), BF16),
        pltpu.VMEM((n, 2 * LANES), BF16),
        pltpu.VMEM((2 * n, 2 * LANES), F32),
        *[stage] * 8,
        pltpu.VMEM((layers * n // 2, LANES), F32),
        pltpu.VMEM((layers * n // 2, LANES), F32),
        pltpu.VMEM((layers * 2 * layers, wide, LANES), F32),
        pltpu.VMEM((32, n), F32),
        pltpu.VMEM((32, n), F32),
        pltpu.VMEM((32, n), F32),
        pltpu.VMEM((CLASSES, LANES), F32),
        pltpu.VMEM((lat, CLASSES, LANES), F32),
        pltpu.VMEM((CLASSES, LANES), F32),
        pltpu.VMEM((freqs, CLASSES, LANES), F32),
        dma((7,)),
        dma((12,)),
        *[dma((ITERS, lat))] * 2,
        *[dma((ITERS, layers))] * 4,
        *[dma((ITERS, lat))] * 2,
        *[dma((layers,))] * 2,
        *[dma((freqs,))] * 2,
        *[dma((lat,))] * 2,
        *[dma((freqs,))] * 4,
    ]
    cell, classes = pl.pallas_call(
        functools.partial(kernel, lat, layers, freqs, n),
        out_shape=(jax.ShapeDtypeStruct((32, n), F32), jax.ShapeDtypeStruct((1, CLASSES), F32)),
        in_specs=[pl.BlockSpec(memory_space=pl.ANY)] * 7,
        out_specs=(pl.BlockSpec(memory_space=pltpu.VMEM), pl.BlockSpec(memory_space=pltpu.VMEM)),
        scratch_shapes=scratch,
        compiler_params=pltpu.CompilerParams(
            collective_id=0, has_side_effects=True
        ),
    )(
        source.reshape(2, 2, 32, n),
        contrast.reshape(2, 32, n),
        green.reshape(2 * layers, 32, n),
        efield.reshape(2, 2, 32, n),
        cell_class.reshape(32, n),
        jnp.asarray(high),
        jnp.asarray(low),
    )
    return cell.reshape(1, 32, n), classes


def solution(mesh):
    placed = (
        P(None, "freq", None, "layer", "lat", None),
        P(None, "freq", "layer", "lat", None),
        P(None, "freq", None, "layer", "lat", None),
        P(None, "freq", None, "layer", "lat", None),
        P("layer", "lat", None),
    )
    sizes = (mesh.shape["lat"], mesh.shape["layer"], mesh.shape["freq"])
    return jax.shard_map(
        functools.partial(per_device, *sizes),
        mesh=mesh,
        in_specs=placed,
        out_specs=(P("layer", "lat", None), P("layer", None)),
        check_vma=False,
    )
```

```python
import functools
import itertools

import jax
import jax.numpy as jnp
import numpy as np
from jax import lax
from jax.experimental import pallas as pl
from jax.experimental.pallas import tpu as pltpu
from jax.sharding import PartitionSpec as P

ITERS = 2
CLASSES = 8
LANES = 128
MESH = pl.DeviceIdType.MESH
F32 = jnp.float32
BF16 = jnp.bfloat16


def tables(length):
    half = np.arange(length // 2)
    phases = (2 * half[:, None] * half[None, :], half[:, None] * (2 * half[None, :] + 1), (2 * half[:, None] + 1) * half[None, :])
    angles = [(phase % length) * (2.0 * np.pi / length) for phase in phases]
    both = np.stack([np.concatenate([np.cos(angle), np.sin(angle)]) for angle in angles]) / np.sqrt(length)
    high = both.astype(BF16)
    low = (both - high.astype(np.float64)).astype(BF16)
    return high, low


def split(value):
    high = value.astype(BF16)
    return high, (value - high.astype(F32)).astype(BF16)


def dot(a, b):
    return jnp.dot(a, b, preferred_element_type=F32)


def lane_of(shape):
    return lax.broadcasted_iota(jnp.int32, shape, len(shape) - 1)


def turn_lanes(parts):
    parts = list(parts)
    lane = lane_of(parts[0].shape)
    for bit in (1, 2, 4):
        width = 16 * bit
        odd = (lane // width) % 2 == 1
        for q in range(8):
            if q & bit == 0:
                first, second = parts[q], parts[q | bit]
                parts[q] = jnp.where(odd, pltpu.roll(second, width, 1), first)
                parts[q | bit] = jnp.where(odd, second, pltpu.roll(first, LANES - width, 1))
    return parts


def turned(value, sign):
    real = (lane_of(value.shape) // 32) % 2 == 0
    return jnp.where(real, -sign * pltpu.roll(value, LANES - 32, 1), sign * pltpu.roll(value, 32, 1))


def butterfly(value):
    return pltpu.roll(value, 64, 1) + jnp.where(lane_of(value.shape) < 64, value, -value)


def kernel(
    lat, layers, freqs, n,
    src_hbm, con_hbm, grn_hbm, efd_hbm, cls_hbm, high_hbm, low_hbm,
    cell_out, class_out,
    src_raw, con_raw, grn, efd, cls, high, low,
    src, con, field, rows_buf, cols_buf, prod,
    send_a, recv_a, send_b, recv_b, send_c, recv_c, send_d, recv_d,
    send_g, recv_g, wide_g,
    terms, recv_t, cell, part, recv_l, part_f, recv_k,
    load_sem, own_sem,
    sa_sem, ra_sem, sb_sem, rb_sem, sc_sem, rc_sem, sd_sem, rd_sem,
    sg_sem, rg_sem, st_sem, rt_sem, sl_sem, rl_sem, su_sem, ru_sem, sk_sem, rk_sem,
):
    at = {"lat": lax.axis_index("lat"), "layer": lax.axis_index("layer"), "freq": lax.axis_index("freq")}
    size = {"lat": lat, "layer": layers, "freq": freqs}
    half = n // 2
    wide = half // layers

    barrier = pltpu.get_barrier_semaphore()
    for axis in ("lat", "layer", "freq"):
        def greet(k, carry, axis=axis):
            peer = lax.rem(at[axis] + k, size[axis])
            pl.semaphore_signal(barrier, inc=1, device_id={axis: peer}, device_id_type=MESH)
            return carry
        lax.fori_loop(1, size[axis], greet, 0)

    tiles = n // LANES

    def by_tile(i, source, target):
        lead = (slice(None),) * (len(source.shape) - 1)
        return [
            pltpu.make_async_copy(source.at[lead + (slice(t * LANES, (t + 1) * LANES),)], target.at[t], load_sem.at[i, t])
            for t in range(tiles)
        ]

    loads = [
        by_tile(0, src_hbm, src_raw),
        by_tile(1, con_hbm, con_raw),
        [pltpu.make_async_copy(high_hbm, high, load_sem.at[2, 0])],
        [pltpu.make_async_copy(low_hbm, low, load_sem.at[3, 0])],
        by_tile(4, grn_hbm, grn),
        by_tile(5, efd_hbm, efd),
        [pltpu.make_async_copy(cls_hbm, cls, load_sem.at[6, 0])],
    ]
    for load in loads:
        for copy in load:
            copy.start()

    def loaded(i):
        for copy in loads[i]:
            copy.wait()

    def remote(axis, peer, source, target, send_sem, recv_sem):
        return pltpu.make_async_remote_copy(
            src_ref=source, dst_ref=target, send_sem=send_sem, recv_sem=recv_sem,
            device_id={axis: peer}, device_id_type=MESH,
        )

    def each_peer(axis, act):
        pair = 1 if axis == "freq" else 2
        ring = size[axis] // pair
        def one(k, carry):
            i = k // pair
            ahead = i % 2
            hop = ahead * (ring // 2 - (i + 1) // 2) + (1 - ahead) * (ring - ring // 2 + i // 2)
            place = lax.rem(at[axis] // pair + hop, ring)
            act(place * pair + (at[axis] + pair - 1 - k % pair) % pair)
            return carry
        lax.fori_loop(0, size[axis] - 1, one, 0)

    def swap(axis, source, target, rows, send_sem, recv_sem, own):
        me = at[axis]
        def block(ref, i):
            return ref.at[pl.ds(pl.multiple_of(i * rows, 8), rows)]
        def copy(peer, landing):
            return remote(axis, peer, block(source, peer), block(target, landing), send_sem.at[peer], recv_sem.at[landing])
        def mine():
            return pltpu.make_async_copy(block(source, me), block(target, me), own)
        def start():
            each_peer(axis, lambda peer: copy(peer, me).start())
            mine().start()
        def arrived():
            each_peer(axis, lambda peer: copy(peer, peer).wait_recv())
            mine().wait()
        def sent():
            each_peer(axis, lambda peer: copy(peer, me).wait_send())
        return start, arrived, sent

    def spread(axis, source, target, send_sem, recv_sem, own):
        me = at[axis]
        def copy(peer, landing):
            return remote(axis, peer, source, target.at[landing], send_sem.at[peer], recv_sem.at[landing])
        def mine():
            return pltpu.make_async_copy(source, target.at[me], own)
        def start():
            each_peer(axis, lambda peer: copy(peer, me).start())
            mine().start()
        def arrived():
            each_peer(axis, lambda peer: copy(peer, peer).wait_recv())
            mine().wait()
        def sent():
            each_peer(axis, lambda peer: copy(peer, me).wait_send())
        return start, arrived, sent

    green_copies = swap("layer", send_g, recv_g, half, sg_sem, rg_sem, own_sem.at[16])

    def exchange(which, step, pol):
        axis, source, target, rows, send_sem, recv_sem = (
            ("lat", send_a, recv_a, 16, sa_sem, ra_sem),
            ("layer", send_b, recv_b, wide, sb_sem, rb_sem),
            ("layer", send_c, recv_c, wide, sc_sem, rc_sem),
            ("lat", send_d, recv_d, 16, sd_sem, rd_sem),
        )[which]
        return swap(
            axis, source.at[step, pol], target.at[step, pol], rows, send_sem.at[step, pol], recv_sem.at[step, pol],
            own_sem.at[(step * 2 + pol) * 4 + which],
        )

    def lane_transform(parity, table):
        whole = rows_buf[parity]
        upper = rows_buf[parity, 0:64]
        out = []
        for base in (0, half):
            product = dot(whole, high[table, base:base + half])
            out.append(product[:64] + product[64:] + dot(upper, low[table, base:base + half]))
        return out

    def row_transform(value, odd_table):
        upper, lower = split(value)
        cols_buf[:, 0:LANES] = upper
        cols_buf[:, LANES:2 * LANES] = lower
        for i, table in enumerate((0, odd_table)):
            prod[i] = dot(high[table], cols_buf[...])
        full = []
        for i, table in enumerate((0, odd_table)):
            tail = dot(low[table], cols_buf[:, 0:LANES])
            full.append(prod[i, :, 0:LANES] + prod[i, :, LANES:2 * LANES] + tail)
        both = jnp.where(lane_of(full[0].shape) < 64, full[0], full[1])
        return both[:half], both[half:]

    def put_rows(parity, row, lanes, value):
        upper, lower = split(value)
        count = value.shape[0]
        rows_buf[parity, row:row + count, lanes] = upper
        rows_buf[parity, 64 + row:64 + row + count, lanes] = lower

    def forward_lanes(step, pol):
        for piece, value in enumerate(
            (
                con[0] * field[0, pol] - con[1] * field[1, pol],
                con[0] * field[1, pol] + con[1] * field[0, pol],
            )
        ):
            put_rows(0, piece * 32, slice(None), value[:, :half] + value[:, half:])
            put_rows(1, piece * 32, slice(None), value[:, :half] - value[:, half:])
        pieces = []
        for parity in range(2):
            cosine, sine = lane_transform(parity, parity)
            pieces.append((cosine[:32] + sine[32:], cosine[32:] - sine[:32]))
        for tile in range(half // LANES):
            lanes = slice(tile * LANES, (tile + 1) * LANES)
            blocks = turn_lanes(
                [pieces[q % 2][q // 2 % 2][q // 4 * 16:q // 4 * 16 + 16, lanes] for q in range(8)]
            )
            for g, block in enumerate(blocks):
                row = (tile * 8 + g) * 16
                send_a[step, pol, row:row + 16] = block

    def inverse_lanes(step, pol):
        for tile in range(half // LANES):
            lanes = slice(tile * LANES, (tile + 1) * LANES)
            blocks = turn_lanes([recv_d[step, pol, pl.ds((tile * 8 + g) * 16, 16)] for g in range(8)])
            for q, block in enumerate(blocks):
                put_rows(q % 2, q // 2 % 2 * 32 + q // 4 * 16, lanes, block)
        pieces = []
        for parity in range(2):
            cosine, sine = lane_transform(parity, 2 * parity)
            pieces.append((cosine[:32] - sine[32:], cosine[32:] + sine[:32]))
        for lanes, sign in ((slice(0, half), 1.0), (slice(half, n), -1.0)):
            real, imag = (pieces[0][i] + sign * pieces[1][i] for i in range(2))
            field[0, pol, :, lanes] = src[0, pol, :, lanes] + con[0, :, lanes] * real - con[1, :, lanes] * imag
            field[1, pol, :, lanes] = src[1, pol, :, lanes] + con[0, :, lanes] * imag + con[1, :, lanes] * real

    def prepare_green():
        loaded(4)
        for pair in range(layers):
            for tile in range(half // LANES):
                rows = [
                    grn[end * (half // LANES) + tile, 2 * pair + s, pl.ds(parity, 16, stride=2)]
                    for end in range(2) for s in range(2) for parity in range(2)
                ]
                flipped = jnp.concatenate(rows, axis=0).T
                for part_of in range(LANES // wide):
                    row = ((tile * LANES // wide + part_of) * layers + pair) * wide
                    send_g[row:row + wide] = flipped[part_of * wide:(part_of + 1) * wide]

    def widen(i, carry):
        value = recv_g[pl.ds(pl.multiple_of(i * wide, 8), wide)]
        odd = (lane_of(value.shape) // 32) % 2 == 1
        wide_g[i * 2] = jnp.where(odd, pltpu.roll(value, 32, 1), value)
        wide_g[i * 2 + 1] = jnp.where(odd, value, pltpu.roll(value, LANES - 32, 1))
        return carry

    def mix(step, pol):
        def rows(r, carry):
            base = pl.multiple_of(r * 8, 8)
            sums = [None] * layers
            for l in range(layers):
                value = recv_b[step, pol, pl.ds(pl.multiple_of(l * wide + base, 8), 8)]
                side = turned(value, 1.0)
                for o in range(layers):
                    term = (
                        wide_g[l * 2 * layers + o, pl.ds(base, 8)] * value
                        + wide_g[l * 2 * layers + layers + o, pl.ds(base, 8)] * side
                    )
                    sums[o] = term if l == 0 else sums[o] + term
            for o in range(layers):
                send_c[step, pol, pl.ds(pl.multiple_of(o * wide + base, 8), 8)] = sums[o]
            return carry

        lax.fori_loop(0, wide // 8, rows, 0)

    even_odd = [(slice(parity * 16, parity * 16 + 16), pl.ds(parity, 16, stride=2)) for parity in range(2)]
    loaded(1)
    for mine, stride in even_odd:
        for piece, t in itertools.product(range(2), range(tiles)):
            con[piece, mine, t * LANES:(t + 1) * LANES] = con_raw[t, piece, stride]
    loaded(0)
    for mine, stride in even_odd:
        for piece, pol, t in itertools.product(range(2), range(2), range(tiles)):
            value = src_raw[t, piece, pol, stride]
            src[piece, pol, mine, t * LANES:(t + 1) * LANES] = value
            field[piece, pol, mine, t * LANES:(t + 1) * LANES] = value
    loaded(2)
    loaded(3)

    def iterate(step, carry):
        for pol in range(2):
            @pl.when(step > 0)
            def _():
                exchange(3, step - 1, pol)[1]()
                inverse_lanes(step - 1, pol)

            forward_lanes(step, pol)

            if pol == 0:
                @pl.when(step == 0)
                def _():
                    pl.semaphore_wait(barrier, lat + layers + freqs - 3)

            exchange(0, step, pol)[0]()

        @pl.when(step == 0)
        def _():
            prepare_green()
            green_copies[0]()

        for pol in range(2):
            exchange(0, step, pol)[1]()
            cosine, sine = row_transform(recv_a[step, pol], 1)
            send_b[step, pol] = butterfly(cosine + turned(sine, -1.0))
            exchange(1, step, pol)[0]()

        @pl.when(step == 0)
        def _():
            green_copies[1]()
            lax.fori_loop(0, layers * layers, widen, 0)

        for pol in range(2):
            exchange(1, step, pol)[1]()
            mix(step, pol)
            exchange(2, step, pol)[0]()

        for pol in range(2):
            exchange(2, step, pol)[1]()
            cosine, sine = row_transform(butterfly(recv_c[step, pol]), 2)
            send_d[step, pol] = cosine + turned(sine, 1.0)
            exchange(3, step, pol)[0]()
        return carry

    lax.fori_loop(0, ITERS, iterate, 0)

    loaded(5)
    loaded(6)
    for pol in range(2):
        exchange(3, ITERS - 1, pol)[1]()
        inverse_lanes(ITERS - 1, pol)
        for parity, t in itertools.product(range(2), range(tiles)):
            mine = slice(parity * 16, parity * 16 + 16)
            lanes = slice(t * LANES, (t + 1) * LANES)
            stride = pl.ds(parity, 16, stride=2)
            value = efd[t, 0, pol, stride] * field[0, pol, mine, lanes] - efd[t, 1, pol, stride] * field[1, pol, mine, lanes]
            spots = pl.ds(t * 32 + parity, 16, stride=2)
            terms[spots] = value if pol == 0 else terms[spots] + value
    own_rows = tiles * 32 // freqs
    scatter = swap("freq", terms, recv_t, own_rows, st_sem, rt_sem, own_sem.at[17])
    scatter[0]()

    for c in range(CLASSES):
        kept = [
            jnp.where(cls[:, t * LANES:(t + 1) * LANES] == c, terms[t * 32:(t + 1) * 32], 0.0) for t in range(tiles)
        ]
        part[c:c + 1] = jnp.sum(sum(kept), axis=0, keepdims=True)
    lat_sums = spread("lat", part, recv_l, sl_sem, rl_sem, own_sem.at[18])
    lat_sums[0]()

    scatter[1]()
    mine = recv_t[0:own_rows]
    for f in range(1, freqs):
        mine = mine + recv_t[f * own_rows:(f + 1) * own_rows]
    own = pl.ds(pl.multiple_of(at["freq"] * own_rows, 8), own_rows)
    cell[own] = mine

    def gather(peer, landing):
        rows = pl.ds(pl.multiple_of(landing * own_rows, 8), own_rows)
        return remote("freq", peer, cell.at[rows], cell.at[rows], su_sem.at[peer], ru_sem.at[landing])

    each_peer("freq", lambda peer: gather(peer, at["freq"]).start())

    lat_sums[1]()
    part_f[...] = jnp.sum(recv_l[...], axis=0)
    freq_sums = spread("freq", part_f, recv_k, sk_sem, rk_sem, own_sem.at[19])
    freq_sums[0]()

    each_peer("freq", lambda peer: gather(peer, peer).wait_recv())
    for t in range(tiles):
        cell_out[:, t * LANES:(t + 1) * LANES] = cell[t * 32:(t + 1) * 32]
    freq_sums[1]()
    sums = jnp.sum(jnp.sum(recv_k[...], axis=0), axis=1, keepdims=True) / float(n)
    spot = lax.broadcasted_iota(jnp.int32, (CLASSES, LANES), 0) == lane_of((CLASSES, LANES))
    class_out[...] = jnp.sum(jnp.where(spot, sums, 0.0), axis=0, keepdims=True)[:, :CLASSES]

    def drain(step, carry):
        for pol in range(2):
            for which in range(4):
                exchange(which, step, pol)[2]()
        return carry

    lax.fori_loop(0, ITERS, drain, 0)
    green_copies[2]()
    scatter[2]()
    lat_sums[2]()
    each_peer("freq", lambda peer: gather(peer, at["freq"]).wait_send())
    freq_sums[2]()


def per_device(lat, layers, freqs, source, contrast, green, efield, cell_class):
    n = source.shape[5]
    high, low = tables(n)
    half = n // 2
    wide = half // layers
    dma = pltpu.SemaphoreType.DMA
    stage = pltpu.VMEM((ITERS, 2, half, LANES), F32)
    tiles = n // LANES
    scratch = [
        pltpu.VMEM((tiles, 2, 2, 32, LANES), F32),
        pltpu.VMEM((tiles, 2, 32, LANES), F32),
        pltpu.VMEM((tiles, 2 * layers, 32, LANES), F32),
        pltpu.VMEM((tiles, 2, 2, 32, LANES), F32),
        pltpu.VMEM((32, n), jnp.int32),
        pltpu.VMEM((3, n, half), BF16),
        pltpu.VMEM((3, n, half), BF16),
        pltpu.VMEM((2, 2, 32, n), F32),
        pltpu.VMEM((2, 32, n), F32),
        pltpu.VMEM((2, 2, 32, n), F32),
        pltpu.VMEM((2, LANES, half), BF16),
        pltpu.VMEM((half, 2 * LANES), BF16),
        pltpu.VMEM((2, n, 2 * LANES), F32),
        *[stage] * 8,
        pltpu.VMEM((layers * half, LANES), F32),
        pltpu.VMEM((layers * half, LANES), F32),
        pltpu.VMEM((layers * 2 * layers, wide, LANES), F32),
        pltpu.VMEM((tiles * 32, LANES), F32),
        pltpu.VMEM((tiles * 32, LANES), F32),
        pltpu.VMEM((tiles * 32, LANES), F32),
        pltpu.VMEM((CLASSES, LANES), F32),
        pltpu.VMEM((lat, CLASSES, LANES), F32),
        pltpu.VMEM((CLASSES, LANES), F32),
        pltpu.VMEM((freqs, CLASSES, LANES), F32),
        dma((7, tiles)),
        dma((20,)),
        *[dma((ITERS, 2, lat))] * 2,
        *[dma((ITERS, 2, layers))] * 4,
        *[dma((ITERS, 2, lat))] * 2,
        *[dma((layers,))] * 2,
        *[dma((freqs,))] * 2,
        *[dma((lat,))] * 2,
        *[dma((freqs,))] * 4,
    ]
    cell, classes = pl.pallas_call(
        functools.partial(kernel, lat, layers, freqs, n),
        out_shape=(jax.ShapeDtypeStruct((32, n), F32), jax.ShapeDtypeStruct((1, CLASSES), F32)),
        in_specs=[pl.BlockSpec(memory_space=pl.ANY)] * 7,
        out_specs=(pl.BlockSpec(memory_space=pltpu.VMEM), pl.BlockSpec(memory_space=pltpu.VMEM)),
        scratch_shapes=scratch,
        compiler_params=pltpu.CompilerParams(
            collective_id=0, has_side_effects=True
        ),
    )(
        source.reshape(2, 2, 32, n),
        contrast.reshape(2, 32, n),
        green.reshape(2 * layers, 32, n),
        efield.reshape(2, 2, 32, n),
        cell_class.reshape(32, n),
        jnp.asarray(high),
        jnp.asarray(low),
    )
    return cell.reshape(1, 32, n), classes


def solution(mesh):
    placed = (
        P(None, "freq", None, "layer", "lat", None),
        P(None, "freq", "layer", "lat", None),
        P(None, "freq", None, "layer", "lat", None),
        P(None, "freq", None, "layer", "lat", None),
        P("layer", "lat", None),
    )
    sizes = (mesh.shape["lat"], mesh.shape["layer"], mesh.shape["freq"])
    return jax.shard_map(
        functools.partial(per_device, *sizes),
        mesh=mesh,
        in_specs=placed,
        out_specs=(P("layer", "lat", None), P("layer", None)),
        check_vma=False,
    )
```

```python
import functools
import itertools

import jax
import jax.numpy as jnp
import numpy as np
from jax import lax
from jax.experimental import pallas as pl
from jax.experimental.pallas import tpu as pltpu
from jax.sharding import PartitionSpec as P

ITERS = 2
CLASSES = 8
LANES = 128
MESH = pl.DeviceIdType.MESH
F32 = jnp.float32
BF16 = jnp.bfloat16


def tables(length):
    half = np.arange(length // 2)
    phases = (2 * half[:, None] * half[None, :], half[:, None] * (2 * half[None, :] + 1), (2 * half[:, None] + 1) * half[None, :])
    angles = [(phase % length) * (2.0 * np.pi / length) for phase in phases]
    both = np.stack([np.concatenate([np.cos(angle), np.sin(angle)]) for angle in angles]) / np.sqrt(length)
    high = both.astype(BF16)
    low = (both - high.astype(np.float64)).astype(BF16)
    return high, low


def split(value):
    high = value.astype(BF16)
    return high, (value - high.astype(F32)).astype(BF16)


def dot(a, b):
    return jnp.dot(a, b, preferred_element_type=F32)


def lane_of(shape):
    return lax.broadcasted_iota(jnp.int32, shape, len(shape) - 1)


def turn_lanes(parts):
    parts = list(parts)
    lane = lane_of(parts[0].shape)
    for bit in (1, 2, 4):
        width = 16 * bit
        odd = (lane // width) % 2 == 1
        for q in range(8):
            if q & bit == 0:
                first, second = parts[q], parts[q | bit]
                parts[q] = jnp.where(odd, pltpu.roll(second, width, 1), first)
                parts[q | bit] = jnp.where(odd, second, pltpu.roll(first, LANES - width, 1))
    return parts


def turned(value, sign):
    real = (lane_of(value.shape) // 32) % 2 == 0
    return jnp.where(real, -sign * pltpu.roll(value, LANES - 32, 1), sign * pltpu.roll(value, 32, 1))


def butterfly(value):
    return pltpu.roll(value, 64, 1) + jnp.where(lane_of(value.shape) < 64, value, -value)


def kernel(
    lat, layers, freqs, n,
    src_hbm, con_hbm, grn_hbm, efd_hbm, cls_hbm, high_hbm, low_hbm,
    cell_out, class_out,
    src_raw, con_raw, grn, efd, cls, high, low,
    src, con, field, rows_buf, cols_buf, prod,
    send_a, recv_a, send_b, recv_b, send_c, recv_c, send_d, recv_d,
    send_g, recv_g, wide_g,
    terms, recv_t, cell, part, recv_l, part_f, recv_k,
    load_sem, own_sem,
    sa_sem, ra_sem, sb_sem, rb_sem, sc_sem, rc_sem, sd_sem, rd_sem,
    sg_sem, rg_sem, st_sem, rt_sem, sl_sem, rl_sem, su_sem, ru_sem, sk_sem, rk_sem,
):
    at = {axis: lax.axis_index(axis) for axis in ("lat", "layer", "freq")}
    size = {"lat": lat, "layer": layers, "freq": freqs}

    def others(axis):
        pair = 1 if axis == "freq" else 2
        ring = size[axis] // pair
        found = []
        for k in range(size[axis] - 1):
            i = k // pair
            hop = ring // 2 - (i + 1) // 2 if i % 2 else ring - ring // 2 + i // 2
            peer = lax.rem(at[axis] // pair + hop, ring) * pair
            if pair == 2:
                side = lax.rem(at[axis], 2)
                peer = peer + (1 - side if k % 2 == 0 else side)
            found.append((peer, {axis: peer}))
        return found

    peers = {axis: others(axis) for axis in at}
    half = n // 2
    wide = half // layers

    barrier = pltpu.get_barrier_semaphore()
    for axis in ("lat", "layer", "freq"):
        for _, device in peers[axis]:
            pl.semaphore_signal(barrier, inc=1, device_id=device, device_id_type=MESH)
    tiles = n // LANES

    def by_tile(i, source, target):
        lead = (slice(None),) * (len(source.shape) - 1)
        return [
            pltpu.make_async_copy(source.at[lead + (slice(t * LANES, (t + 1) * LANES),)], target.at[t], load_sem.at[i, t])
            for t in range(tiles)
        ]

    loads = [
        by_tile(0, src_hbm, src_raw),
        by_tile(1, con_hbm, con_raw),
        [pltpu.make_async_copy(high_hbm, high, load_sem.at[2, 0])],
        [pltpu.make_async_copy(low_hbm, low, load_sem.at[3, 0])],
        by_tile(4, grn_hbm, grn),
        by_tile(5, efd_hbm, efd),
        [pltpu.make_async_copy(cls_hbm, cls, load_sem.at[6, 0])],
    ]
    for load in loads:
        for copy in load:
            copy.start()

    def loaded(i):
        for copy in loads[i]:
            copy.wait()

    def remote(device, source, target, send_sem, recv_sem):
        return pltpu.make_async_remote_copy(
            src_ref=source, dst_ref=target, send_sem=send_sem, recv_sem=recv_sem,
            device_id=device, device_id_type=MESH,
        )

    def trade(axis, outgoing, landing, whole, mine, send_sem, recv_sem):
        def everything():
            return remote(peers[axis][0][1], whole[0], whole[1], send_sem, recv_sem)
        def start():
            for peer, device in peers[axis]:
                remote(device, outgoing(peer), landing, send_sem, recv_sem).start()
            if mine is not None:
                mine().start()
        def arrived():
            if peers[axis]:
                everything().wait_recv()
            if mine is not None:
                mine().wait()
        def sent():
            if peers[axis]:
                everything().wait_send()
        return start, arrived, sent

    def swap(axis, source, target, rows, send_sem, recv_sem, own):
        def block(ref, i):
            return ref.at[pl.ds(pl.multiple_of(i * rows, 8), rows)]
        def mine():
            return pltpu.make_async_copy(block(source, at[axis]), block(target, at[axis]), own)
        whole = tuple(ref.at[pl.ds(0, (size[axis] - 1) * rows)] for ref in (source, target))
        return trade(axis, lambda peer: block(source, peer), block(target, at[axis]), whole, mine, send_sem, recv_sem)

    def spread(axis, source, target, send_sem, recv_sem, own):
        def mine():
            return pltpu.make_async_copy(source, target.at[at[axis]], own)
        whole = (target.at[pl.ds(0, size[axis] - 1)],) * 2
        return trade(axis, lambda peer: source, target.at[at[axis]], whole, mine, send_sem, recv_sem)

    green_copies = swap("layer", send_g, recv_g, half, sg_sem.at[0], rg_sem.at[0], own_sem.at[16])

    def exchange(which, step, pol):
        axis, source, target, rows, send_sem, recv_sem = (
            ("lat", send_a, recv_a, 16, sa_sem, ra_sem),
            ("layer", send_b, recv_b, wide, sb_sem, rb_sem),
            ("layer", send_c, recv_c, wide, sc_sem, rc_sem),
            ("lat", send_d, recv_d, 16, sd_sem, rd_sem),
        )[which]
        return swap(
            axis, source.at[step, pol], target.at[step, pol], rows, send_sem.at[step, pol], recv_sem.at[step, pol],
            own_sem.at[(step * 2 + pol) * 4 + which],
        )

    def lane_transform(parity, table):
        whole = rows_buf[parity]
        upper = rows_buf[parity, 0:64]
        out = []
        for base in (0, half):
            product = dot(whole, high[table, base:base + half])
            out.append(product[:64] + product[64:] + dot(upper, low[table, base:base + half]))
        return out

    def row_transform(value, odd_table):
        upper, lower = split(value)
        cols_buf[:, 0:LANES] = upper
        cols_buf[:, LANES:2 * LANES] = lower
        for i, table in enumerate((0, odd_table)):
            prod[i] = dot(high[table], cols_buf[...])
        full = []
        for i, table in enumerate((0, odd_table)):
            tail = dot(low[table], cols_buf[:, 0:LANES])
            full.append(prod[i, :, 0:LANES] + prod[i, :, LANES:2 * LANES] + tail)
        both = jnp.where(lane_of(full[0].shape) < 64, full[0], full[1])
        return both[:half], both[half:]

    def put_rows(parity, row, lanes, value):
        upper, lower = split(value)
        count = value.shape[0]
        rows_buf[parity, row:row + count, lanes] = upper
        rows_buf[parity, 64 + row:64 + row + count, lanes] = lower

    def forward_lanes(step, pol):
        for piece, value in enumerate(
            (
                con[0] * field[0, pol] - con[1] * field[1, pol],
                con[0] * field[1, pol] + con[1] * field[0, pol],
            )
        ):
            put_rows(0, piece * 32, slice(None), value[:, :half] + value[:, half:])
            put_rows(1, piece * 32, slice(None), value[:, :half] - value[:, half:])
        pieces = []
        for parity in range(2):
            cosine, sine = lane_transform(parity, parity)
            pieces.append((cosine[:32] + sine[32:], cosine[32:] - sine[:32]))
        for tile in range(half // LANES):
            lanes = slice(tile * LANES, (tile + 1) * LANES)
            blocks = turn_lanes(
                [pieces[q % 2][q // 2 % 2][q // 4 * 16:q // 4 * 16 + 16, lanes] for q in range(8)]
            )
            for g, block in enumerate(blocks):
                row = (tile * 8 + g) * 16
                send_a[step, pol, row:row + 16] = block

    def inverse_lanes(step, pol):
        for tile in range(half // LANES):
            lanes = slice(tile * LANES, (tile + 1) * LANES)
            blocks = turn_lanes([recv_d[step, pol, pl.ds((tile * 8 + g) * 16, 16)] for g in range(8)])
            for q, block in enumerate(blocks):
                put_rows(q % 2, q // 2 % 2 * 32 + q // 4 * 16, lanes, block)
        pieces = []
        for parity in range(2):
            cosine, sine = lane_transform(parity, 2 * parity)
            pieces.append((cosine[:32] - sine[32:], cosine[32:] + sine[:32]))
        for lanes, sign in ((slice(0, half), 1.0), (slice(half, n), -1.0)):
            real, imag = (pieces[0][i] + sign * pieces[1][i] for i in range(2))
            field[0, pol, :, lanes] = src[0, pol, :, lanes] + con[0, :, lanes] * real - con[1, :, lanes] * imag
            field[1, pol, :, lanes] = src[1, pol, :, lanes] + con[0, :, lanes] * imag + con[1, :, lanes] * real

    def prepare_green():
        loaded(4)
        for pair in range(layers):
            for tile in range(half // LANES):
                rows = [
                    grn[end * (half // LANES) + tile, 2 * pair + s, pl.ds(parity, 16, stride=2)]
                    for end in range(2) for s in range(2) for parity in range(2)
                ]
                flipped = jnp.concatenate(rows, axis=0).T
                for part_of in range(LANES // wide):
                    row = ((tile * LANES // wide + part_of) * layers + pair) * wide
                    send_g[row:row + wide] = flipped[part_of * wide:(part_of + 1) * wide]

    def widen(i, carry):
        value = recv_g[pl.ds(pl.multiple_of(i * wide, 8), wide)]
        odd = (lane_of(value.shape) // 32) % 2 == 1
        wide_g[i * 2] = jnp.where(odd, pltpu.roll(value, 32, 1), value)
        wide_g[i * 2 + 1] = jnp.where(odd, value, pltpu.roll(value, LANES - 32, 1))
        return carry

    def mix(step, pol):
        def rows(r, carry):
            base = pl.multiple_of(r * 8, 8)
            sums = [None] * layers
            for l in range(layers):
                value = recv_b[step, pol, pl.ds(pl.multiple_of(l * wide + base, 8), 8)]
                side = turned(value, 1.0)
                for o in range(layers):
                    term = (
                        wide_g[l * 2 * layers + o, pl.ds(base, 8)] * value
                        + wide_g[l * 2 * layers + layers + o, pl.ds(base, 8)] * side
                    )
                    sums[o] = term if l == 0 else sums[o] + term
            for o in range(layers):
                send_c[step, pol, pl.ds(pl.multiple_of(o * wide + base, 8), 8)] = sums[o]
            return carry

        lax.fori_loop(0, wide // 8, rows, 0)

    even_odd = [(slice(parity * 16, parity * 16 + 16), pl.ds(parity, 16, stride=2)) for parity in range(2)]
    loaded(1)
    for mine, stride in even_odd:
        for piece, t in itertools.product(range(2), range(tiles)):
            con[piece, mine, t * LANES:(t + 1) * LANES] = con_raw[t, piece, stride]
    loaded(0)
    for mine, stride in even_odd:
        for piece, pol, t in itertools.product(range(2), range(2), range(tiles)):
            value = src_raw[t, piece, pol, stride]
            src[piece, pol, mine, t * LANES:(t + 1) * LANES] = value
            field[piece, pol, mine, t * LANES:(t + 1) * LANES] = value
    loaded(2)
    loaded(3)

    def iterate(step, carry):
        for pol in range(2):
            @pl.when(step > 0)
            def _():
                exchange(3, step - 1, pol)[1]()
                inverse_lanes(step - 1, pol)

            forward_lanes(step, pol)

            if pol == 0:
                @pl.when(step == 0)
                def _():
                    prepare_green()
                    pl.semaphore_wait(barrier, lat + layers + freqs - 3)

            exchange(0, step, pol)[0]()

            if pol == 0:
                @pl.when(step == 0)
                def _():
                    green_copies[0]()

        for pol in range(2):
            exchange(0, step, pol)[1]()
            cosine, sine = row_transform(recv_a[step, pol], 1)
            send_b[step, pol] = butterfly(cosine + turned(sine, -1.0))
            exchange(1, step, pol)[0]()

        @pl.when(step == 0)
        def _():
            green_copies[1]()
            lax.fori_loop(0, layers * layers, widen, 0)

        for pol in range(2):
            exchange(1, step, pol)[1]()
            mix(step, pol)
            exchange(2, step, pol)[0]()

        for pol in range(2):
            exchange(2, step, pol)[1]()
            cosine, sine = row_transform(butterfly(recv_c[step, pol]), 2)
            send_d[step, pol] = cosine + turned(sine, 1.0)
            exchange(3, step, pol)[0]()
        return carry

    lax.fori_loop(0, ITERS, iterate, 0)

    loaded(5)
    loaded(6)
    for pol in range(2):
        exchange(3, ITERS - 1, pol)[1]()
        inverse_lanes(ITERS - 1, pol)
        for parity, t in itertools.product(range(2), range(tiles)):
            mine = slice(parity * 16, parity * 16 + 16)
            lanes = slice(t * LANES, (t + 1) * LANES)
            stride = pl.ds(parity, 16, stride=2)
            value = efd[t, 0, pol, stride] * field[0, pol, mine, lanes] - efd[t, 1, pol, stride] * field[1, pol, mine, lanes]
            spots = pl.ds(t * 32 + parity, 16, stride=2)
            terms[spots] = value if pol == 0 else terms[spots] + value
    own_rows = tiles * 32 // freqs
    scatter = swap("freq", terms, recv_t, own_rows, st_sem.at[0], rt_sem.at[0], own_sem.at[17])
    scatter[0]()

    for c in range(CLASSES):
        kept = [
            jnp.where(cls[:, t * LANES:(t + 1) * LANES] == c, terms[t * 32:(t + 1) * 32], 0.0) for t in range(tiles)
        ]
        part[c:c + 1] = jnp.sum(sum(kept), axis=0, keepdims=True)
    lat_sums = spread("lat", part, recv_l, sl_sem.at[0], rl_sem.at[0], own_sem.at[18])
    lat_sums[0]()

    scatter[1]()
    mine = recv_t[0:own_rows]
    for f in range(1, freqs):
        mine = mine + recv_t[f * own_rows:(f + 1) * own_rows]
    own = pl.ds(pl.multiple_of(at["freq"] * own_rows, 8), own_rows)
    cell[own] = mine

    spots = tuple(cell.at[pl.ds(0, (freqs - 1) * own_rows)] for _ in range(2))
    gather = trade("freq", lambda peer: cell.at[own], cell.at[own], spots, None, su_sem.at[0], ru_sem.at[0])
    gather[0]()

    lat_sums[1]()
    part_f[...] = jnp.sum(recv_l[...], axis=0)
    freq_sums = spread("freq", part_f, recv_k, sk_sem.at[0], rk_sem.at[0], own_sem.at[19])
    freq_sums[0]()

    gather[1]()
    for t in range(tiles):
        cell_out[:, t * LANES:(t + 1) * LANES] = cell[t * 32:(t + 1) * 32]
    freq_sums[1]()
    sums = jnp.sum(jnp.sum(recv_k[...], axis=0), axis=1, keepdims=True) / float(n)
    spot = lax.broadcasted_iota(jnp.int32, (CLASSES, LANES), 0) == lane_of((CLASSES, LANES))
    class_out[...] = jnp.sum(jnp.where(spot, sums, 0.0), axis=0, keepdims=True)[:, :CLASSES]

    def drain(step, carry):
        for pol in range(2):
            for which in range(4):
                exchange(which, step, pol)[2]()
        return carry

    lax.fori_loop(0, ITERS, drain, 0)
    green_copies[2]()
    scatter[2]()
    lat_sums[2]()
    gather[2]()
    freq_sums[2]()


def per_device(lat, layers, freqs, source, contrast, green, efield, cell_class):
    n = source.shape[5]
    high, low = tables(n)
    half = n // 2
    wide = half // layers
    dma = pltpu.SemaphoreType.DMA
    stage = pltpu.VMEM((ITERS, 2, half, LANES), F32)
    tiles = n // LANES
    scratch = [
        pltpu.VMEM((tiles, 2, 2, 32, LANES), F32),
        pltpu.VMEM((tiles, 2, 32, LANES), F32),
        pltpu.VMEM((tiles, 2 * layers, 32, LANES), F32),
        pltpu.VMEM((tiles, 2, 2, 32, LANES), F32),
        pltpu.VMEM((32, n), jnp.int32),
        pltpu.VMEM((3, n, half), BF16),
        pltpu.VMEM((3, n, half), BF16),
        pltpu.VMEM((2, 2, 32, n), F32),
        pltpu.VMEM((2, 32, n), F32),
        pltpu.VMEM((2, 2, 32, n), F32),
        pltpu.VMEM((2, LANES, half), BF16),
        pltpu.VMEM((half, 2 * LANES), BF16),
        pltpu.VMEM((2, n, 2 * LANES), F32),
        *[stage] * 8,
        pltpu.VMEM((layers * half, LANES), F32),
        pltpu.VMEM((layers * half, LANES), F32),
        pltpu.VMEM((layers * 2 * layers, wide, LANES), F32),
        pltpu.VMEM((tiles * 32, LANES), F32),
        pltpu.VMEM((tiles * 32, LANES), F32),
        pltpu.VMEM((tiles * 32, LANES), F32),
        pltpu.VMEM((CLASSES, LANES), F32),
        pltpu.VMEM((lat, CLASSES, LANES), F32),
        pltpu.VMEM((CLASSES, LANES), F32),
        pltpu.VMEM((freqs, CLASSES, LANES), F32),
        dma((7, tiles)),
        dma((20,)),
        *[dma((ITERS, 2))] * 8,
        *[dma((1,))] * 10,
    ]
    cell, classes = pl.pallas_call(
        functools.partial(kernel, lat, layers, freqs, n),
        out_shape=(jax.ShapeDtypeStruct((32, n), F32), jax.ShapeDtypeStruct((1, CLASSES), F32)),
        in_specs=[pl.BlockSpec(memory_space=pl.ANY)] * 7,
        out_specs=(pl.BlockSpec(memory_space=pltpu.VMEM), pl.BlockSpec(memory_space=pltpu.VMEM)),
        scratch_shapes=scratch,
        compiler_params=pltpu.CompilerParams(
            collective_id=0, has_side_effects=True
        ),
    )(
        source.reshape(2, 2, 32, n),
        contrast.reshape(2, 32, n),
        green.reshape(2 * layers, 32, n),
        efield.reshape(2, 2, 32, n),
        cell_class.reshape(32, n),
        jnp.asarray(high),
        jnp.asarray(low),
    )
    return cell.reshape(1, 32, n), classes


def solution(mesh):
    placed = (
        P(None, "freq", None, "layer", "lat", None),
        P(None, "freq", "layer", "lat", None),
        P(None, "freq", None, "layer", "lat", None),
        P(None, "freq", None, "layer", "lat", None),
        P("layer", "lat", None),
    )
    sizes = (mesh.shape["lat"], mesh.shape["layer"], mesh.shape["freq"])
    return jax.shard_map(
        functools.partial(per_device, *sizes),
        mesh=mesh,
        in_specs=placed,
        out_specs=(P("layer", "lat", None), P("layer", None)),
        check_vma=False,
    )
```

```python
import functools
import itertools

import jax
import jax.numpy as jnp
import numpy as np
from jax import lax
from jax.experimental import pallas as pl
from jax.experimental.pallas import tpu as pltpu
from jax.sharding import PartitionSpec as P

ITERS = 2
CLASSES = 8
LANES = 128
MESH = pl.DeviceIdType.MESH
F32 = jnp.float32
BF16 = jnp.bfloat16


def tables(length):
    half = np.arange(length // 2)
    phases = (2 * half[:, None] * half[None, :], half[:, None] * (2 * half[None, :] + 1), (2 * half[:, None] + 1) * half[None, :])
    angles = [(phase % length) * (2.0 * np.pi / length) for phase in phases]
    both = np.stack([np.concatenate([np.cos(angle), np.sin(angle)]) for angle in angles]) / np.sqrt(length)
    high = both.astype(BF16)
    low = (both - high.astype(np.float64)).astype(BF16)
    return high, low


def split(value):
    high = value.astype(BF16)
    return high, (value - high.astype(F32)).astype(BF16)


def dot(a, b):
    return jnp.dot(a, b, preferred_element_type=F32)


def lane_of(shape):
    return lax.broadcasted_iota(jnp.int32, shape, len(shape) - 1)


def turn_lanes(parts):
    parts = list(parts)
    lane = lane_of(parts[0].shape)
    for bit in (1, 2, 4):
        width = 16 * bit
        odd = (lane // width) % 2 == 1
        for q in range(8):
            if q & bit == 0:
                first, second = parts[q], parts[q | bit]
                parts[q] = jnp.where(odd, pltpu.roll(second, width, 1), first)
                parts[q | bit] = jnp.where(odd, second, pltpu.roll(first, LANES - width, 1))
    return parts


def turned(value, sign):
    real = (lane_of(value.shape) // 32) % 2 == 0
    return jnp.where(real, -sign * pltpu.roll(value, LANES - 32, 1), sign * pltpu.roll(value, 32, 1))


def butterfly(value):
    return pltpu.roll(value, 64, 1) + jnp.where(lane_of(value.shape) < 64, value, -value)


def kernel(
    lat, layers, freqs, n,
    src_hbm, con_hbm, grn_hbm, efd_hbm, cls_hbm, high_hbm, low_hbm,
    cell_out, class_out,
    src_raw, con_raw, grn, efd, cls, high, low,
    src, con, field, rows_buf, cols_buf, prod,
    send_a, recv_a, send_b, recv_b, send_c, recv_c, send_d, recv_d,
    send_g, recv_g, wide_g,
    terms, recv_t, cell, lines, part, recv_l, part_f, recv_k,
    load_sem, own_sem,
    sa_sem, ra_sem, sb_sem, rb_sem, sc_sem, rc_sem, sd_sem, rd_sem,
    sg_sem, rg_sem, st_sem, rt_sem, sl_sem, rl_sem, su_sem, ru_sem, sk_sem, rk_sem,
):
    at = {axis: lax.axis_index(axis) for axis in ("lat", "layer", "freq")}
    size = {"lat": lat, "layer": layers, "freq": freqs}

    def others(axis):
        pair = 1 if axis == "freq" else 2
        ring = size[axis] // pair
        found = []
        for k in range(size[axis] - 1):
            i = k // pair
            hop = ring // 2 - (i + 1) // 2 if i % 2 else ring - ring // 2 + i // 2
            peer = lax.rem(at[axis] // pair + hop, ring) * pair
            if pair == 2:
                side = lax.rem(at[axis], 2)
                peer = peer + (1 - side if k % 2 == 0 else side)
            found.append((peer, {axis: peer}))
        return found

    peers = {axis: others(axis) for axis in at}
    half = n // 2
    wide = half // layers

    barrier = pltpu.get_barrier_semaphore()
    for axis in ("lat", "layer", "freq"):
        for _, device in peers[axis]:
            pl.semaphore_signal(barrier, inc=1, device_id=device, device_id_type=MESH)
    tiles = n // LANES

    def by_tile(i, source, target):
        lead = (slice(None),) * (len(source.shape) - 1)
        return [
            pltpu.make_async_copy(source.at[lead + (slice(t * LANES, (t + 1) * LANES),)], target.at[t], load_sem.at[i, t])
            for t in range(tiles)
        ]

    loads = [
        by_tile(0, src_hbm, src_raw),
        by_tile(1, con_hbm, con_raw),
        [pltpu.make_async_copy(high_hbm, high, load_sem.at[2, 0])],
        [pltpu.make_async_copy(low_hbm, low, load_sem.at[3, 0])],
        by_tile(4, grn_hbm, grn),
        by_tile(5, efd_hbm, efd),
        [pltpu.make_async_copy(cls_hbm, cls, load_sem.at[6, 0])],
    ]
    for load in loads:
        for copy in load:
            copy.start()

    def loaded(i):
        for copy in loads[i]:
            copy.wait()

    def remote(device, source, target, send_sem, recv_sem):
        return pltpu.make_async_remote_copy(
            src_ref=source, dst_ref=target, send_sem=send_sem, recv_sem=recv_sem,
            device_id=device, device_id_type=MESH,
        )

    def trade(axis, outgoing, landing, whole, mine, send_sem, recv_sem):
        def everything():
            return remote(peers[axis][0][1], whole[0], whole[1], send_sem, recv_sem)
        def start():
            for peer, device in peers[axis]:
                remote(device, outgoing(peer), landing, send_sem, recv_sem).start()
            if mine is not None:
                mine().start()
        def arrived():
            if peers[axis]:
                everything().wait_recv()
            if mine is not None:
                mine().wait()
        def sent():
            if peers[axis]:
                everything().wait_send()
        return start, arrived, sent

    def swap(axis, source, target, rows, send_sem, recv_sem, own):
        def block(ref, i):
            return ref.at[pl.ds(pl.multiple_of(i * rows, 8), rows)]
        def mine():
            return pltpu.make_async_copy(block(source, at[axis]), block(target, at[axis]), own)
        whole = tuple(ref.at[pl.ds(0, (size[axis] - 1) * rows)] for ref in (source, target))
        return trade(axis, lambda peer: block(source, peer), block(target, at[axis]), whole, mine, send_sem, recv_sem)

    def spread(axis, source, target, send_sem, recv_sem, own):
        def mine():
            return pltpu.make_async_copy(source, target.at[at[axis]], own)
        whole = (target.at[pl.ds(0, size[axis] - 1)],) * 2
        return trade(axis, lambda peer: source, target.at[at[axis]], whole, mine, send_sem, recv_sem)

    def green_block(ref, i):
        return ref.at[pl.ds(pl.multiple_of(i * half, 8), half)]

    def green_copy(device, peer, slot):
        return remote(device, green_block(send_g, peer), green_block(recv_g, slot), sg_sem.at[0], rg_sem.at[slot])

    def exchange(which, step, pol):
        axis, source, target, rows, send_sem, recv_sem = (
            ("lat", send_a, recv_a, 16, sa_sem, ra_sem),
            ("layer", send_b, recv_b, wide, sb_sem, rb_sem),
            ("layer", send_c, recv_c, wide, sc_sem, rc_sem),
            ("lat", send_d, recv_d, 16, sd_sem, rd_sem),
        )[which]
        return swap(
            axis, source.at[step, pol], target.at[step, pol], rows, send_sem.at[step, pol], recv_sem.at[step, pol],
            own_sem.at[(step * 2 + pol) * 4 + which],
        )

    def lane_transform(parity, table):
        whole = rows_buf[parity]
        upper = rows_buf[parity, 0:64]
        out = []
        for base in (0, half):
            product = dot(whole, high[table, base:base + half])
            out.append(product[:64] + product[64:] + dot(upper, low[table, base:base + half]))
        return out

    def row_transform(value, odd_table):
        upper, lower = split(value)
        cols_buf[:, 0:LANES] = upper
        cols_buf[:, LANES:2 * LANES] = lower
        for i, table in enumerate((0, odd_table)):
            prod[i] = dot(high[table], cols_buf[...])
        full = []
        for i, table in enumerate((0, odd_table)):
            tail = dot(low[table], cols_buf[:, 0:LANES])
            full.append(prod[i, :, 0:LANES] + prod[i, :, LANES:2 * LANES] + tail)
        both = jnp.where(lane_of(full[0].shape) < 64, full[0], full[1])
        return both[:half], both[half:]

    def put_rows(parity, row, lanes, value):
        upper, lower = split(value)
        count = value.shape[0]
        rows_buf[parity, row:row + count, lanes] = upper
        rows_buf[parity, 64 + row:64 + row + count, lanes] = lower

    def forward_lanes(step, pol):
        for piece, value in enumerate(
            (
                con[0] * field[0, pol] - con[1] * field[1, pol],
                con[0] * field[1, pol] + con[1] * field[0, pol],
            )
        ):
            put_rows(0, piece * 32, slice(None), value[:, :half] + value[:, half:])
            put_rows(1, piece * 32, slice(None), value[:, :half] - value[:, half:])
        pieces = []
        for parity in range(2):
            cosine, sine = lane_transform(parity, parity)
            pieces.append((cosine[:32] + sine[32:], cosine[32:] - sine[:32]))
        for tile in range(half // LANES):
            lanes = slice(tile * LANES, (tile + 1) * LANES)
            blocks = turn_lanes(
                [pieces[q % 2][q // 2 % 2][q // 4 * 16:q // 4 * 16 + 16, lanes] for q in range(8)]
            )
            for g, block in enumerate(blocks):
                row = (tile * 8 + g) * 16
                send_a[step, pol, row:row + 16] = block

    def inverse_lanes(step, pol):
        for tile in range(half // LANES):
            lanes = slice(tile * LANES, (tile + 1) * LANES)
            blocks = turn_lanes([recv_d[step, pol, pl.ds((tile * 8 + g) * 16, 16)] for g in range(8)])
            for q, block in enumerate(blocks):
                put_rows(q % 2, q // 2 % 2 * 32 + q // 4 * 16, lanes, block)
        pieces = []
        for parity in range(2):
            cosine, sine = lane_transform(parity, 2 * parity)
            pieces.append((cosine[:32] - sine[32:], cosine[32:] + sine[:32]))
        for lanes, sign in ((slice(0, half), 1.0), (slice(half, n), -1.0)):
            real, imag = (pieces[0][i] + sign * pieces[1][i] for i in range(2))
            field[0, pol, :, lanes] = src[0, pol, :, lanes] + con[0, :, lanes] * real - con[1, :, lanes] * imag
            field[1, pol, :, lanes] = src[1, pol, :, lanes] + con[0, :, lanes] * imag + con[1, :, lanes] * real

    def prepare_green():
        loaded(4)
        for pair in range(layers):
            for tile in range(half // LANES):
                rows = [
                    grn[end * (half // LANES) + tile, 2 * pair + s, pl.ds(parity, 16, stride=2)]
                    for end in range(2) for s in range(2) for parity in range(2)
                ]
                flipped = jnp.concatenate(rows, axis=0).T
                for part_of in range(LANES // wide):
                    row = ((tile * LANES // wide + part_of) * layers + pair) * wide
                    send_g[row:row + wide] = flipped[part_of * wide:(part_of + 1) * wide]

    def widen(source, l):
        def one(pair, carry):
            value = source[pl.ds(pl.multiple_of((l * layers + pair) * wide, 8), wide)]
            odd = (lane_of(value.shape) // 32) % 2 == 1
            spot = (l * layers + pair) * 2
            wide_g[spot] = jnp.where(odd, pltpu.roll(value, 32, 1), value)
            wide_g[spot + 1] = jnp.where(odd, value, pltpu.roll(value, LANES - 32, 1))
            return carry
        lax.fori_loop(0, layers, one, 0)

    def mix(step, pol):
        def rows(r, carry):
            base = pl.multiple_of(r * 8, 8)
            sums = [None] * layers
            for l in range(layers):
                value = recv_b[step, pol, pl.ds(pl.multiple_of(l * wide + base, 8), 8)]
                side = turned(value, 1.0)
                for o in range(layers):
                    term = (
                        wide_g[l * 2 * layers + o, pl.ds(base, 8)] * value
                        + wide_g[l * 2 * layers + layers + o, pl.ds(base, 8)] * side
                    )
                    sums[o] = term if l == 0 else sums[o] + term
            for o in range(layers):
                send_c[step, pol, pl.ds(pl.multiple_of(o * wide + base, 8), 8)] = sums[o]
            return carry

        lax.fori_loop(0, wide // 8, rows, 0)

    even_odd = [(slice(parity * 16, parity * 16 + 16), pl.ds(parity, 16, stride=2)) for parity in range(2)]
    loaded(1)
    for mine, stride in even_odd:
        for piece, t in itertools.product(range(2), range(tiles)):
            con[piece, mine, t * LANES:(t + 1) * LANES] = con_raw[t, piece, stride]
    loaded(0)
    for mine, stride in even_odd:
        for piece, pol, t in itertools.product(range(2), range(2), range(tiles)):
            value = src_raw[t, piece, pol, stride]
            src[piece, pol, mine, t * LANES:(t + 1) * LANES] = value
            field[piece, pol, mine, t * LANES:(t + 1) * LANES] = value
    loaded(2)
    loaded(3)

    def iterate(step, carry):
        for pol in range(2):
            @pl.when(step > 0)
            def _():
                exchange(3, step - 1, pol)[1]()
                inverse_lanes(step - 1, pol)

            forward_lanes(step, pol)

            if pol == 0:
                @pl.when(step == 0)
                def _():
                    prepare_green()
                    pl.semaphore_wait(barrier, lat + layers + freqs - 3)

            exchange(0, step, pol)[0]()

            if pol == 0:
                @pl.when(step == 0)
                def _():
                    for peer, device in peers["layer"]:
                        green_copy(device, peer, at["layer"]).start()

        for pol in range(2):
            exchange(0, step, pol)[1]()
            cosine, sine = row_transform(recv_a[step, pol], 1)
            send_b[step, pol] = butterfly(cosine + turned(sine, -1.0))
            exchange(1, step, pol)[0]()

        @pl.when(step == 0)
        def _():
            widen(send_g, at["layer"])
            for peer, device in peers["layer"]:
                green_copy(device, peer, peer).wait_recv()
                widen(recv_g, peer)

        for pol in range(2):
            exchange(1, step, pol)[1]()
            mix(step, pol)
            exchange(2, step, pol)[0]()

        for pol in range(2):
            exchange(2, step, pol)[1]()
            cosine, sine = row_transform(butterfly(recv_c[step, pol]), 2)
            send_d[step, pol] = cosine + turned(sine, 1.0)
            exchange(3, step, pol)[0]()
        return carry

    lax.fori_loop(0, ITERS, iterate, 0)

    loaded(5)
    loaded(6)
    for pol in range(2):
        exchange(3, ITERS - 1, pol)[1]()
        inverse_lanes(ITERS - 1, pol)
        for parity, t in itertools.product(range(2), range(tiles)):
            mine = slice(parity * 16, parity * 16 + 16)
            lanes = slice(t * LANES, (t + 1) * LANES)
            stride = pl.ds(parity, 16, stride=2)
            value = efd[t, 0, pol, stride] * field[0, pol, mine, lanes] - efd[t, 1, pol, stride] * field[1, pol, mine, lanes]
            spots = pl.ds(t * 32 + parity, 16, stride=2)
            terms[spots] = value if pol == 0 else terms[spots] + value
    own_rows = tiles * 32 // freqs
    scatter = swap("freq", terms, recv_t, own_rows, st_sem.at[0], rt_sem.at[0], own_sem.at[17])
    scatter[0]()

    for c in range(CLASSES):
        kept = [
            jnp.where(cls[:, t * LANES:(t + 1) * LANES] == c, terms[t * 32:(t + 1) * 32], 0.0) for t in range(tiles)
        ]
        lines[c:c + 1] = jnp.sum(sum(kept), axis=0, keepdims=True)
    sums = jnp.sum(lines[...], axis=1, keepdims=True)
    spot = lax.broadcasted_iota(jnp.int32, (CLASSES, LANES), 0) == lane_of((CLASSES, LANES))
    part[...] = jnp.sum(jnp.where(spot, sums, 0.0), axis=0, keepdims=True)
    lat_sums = spread("lat", part, recv_l, sl_sem.at[0], rl_sem.at[0], own_sem.at[18])
    lat_sums[0]()

    scatter[1]()
    mine = recv_t[0:own_rows]
    for f in range(1, freqs):
        mine = mine + recv_t[f * own_rows:(f + 1) * own_rows]
    own = pl.ds(pl.multiple_of(at["freq"] * own_rows, 8), own_rows)
    cell[own] = mine

    spots = tuple(cell.at[pl.ds(0, (freqs - 1) * own_rows)] for _ in range(2))
    gather = trade("freq", lambda peer: cell.at[own], cell.at[own], spots, None, su_sem.at[0], ru_sem.at[0])
    gather[0]()

    lat_sums[1]()
    part_f[...] = jnp.sum(recv_l[...], axis=0)
    freq_sums = spread("freq", part_f, recv_k, sk_sem.at[0], rk_sem.at[0], own_sem.at[19])
    freq_sums[0]()

    gather[1]()
    for t in range(tiles):
        cell_out[:, t * LANES:(t + 1) * LANES] = cell[t * 32:(t + 1) * 32]
    freq_sums[1]()
    class_out[...] = (jnp.sum(recv_k[...], axis=0) / float(n))[:, :CLASSES]

    def drain(step, carry):
        for pol in range(2):
            for which in range(4):
                exchange(which, step, pol)[2]()
        return carry

    lax.fori_loop(0, ITERS, drain, 0)
    for peer, device in peers["layer"]:
        green_copy(device, peer, at["layer"]).wait_send()
    scatter[2]()
    lat_sums[2]()
    gather[2]()
    freq_sums[2]()


def per_device(lat, layers, freqs, source, contrast, green, efield, cell_class):
    n = source.shape[5]
    high, low = tables(n)
    half = n // 2
    wide = half // layers
    dma = pltpu.SemaphoreType.DMA
    stage = pltpu.VMEM((ITERS, 2, half, LANES), F32)
    tiles = n // LANES
    scratch = [
        pltpu.VMEM((tiles, 2, 2, 32, LANES), F32),
        pltpu.VMEM((tiles, 2, 32, LANES), F32),
        pltpu.VMEM((tiles, 2 * layers, 32, LANES), F32),
        pltpu.VMEM((tiles, 2, 2, 32, LANES), F32),
        pltpu.VMEM((32, n), jnp.int32),
        pltpu.VMEM((3, n, half), BF16),
        pltpu.VMEM((3, n, half), BF16),
        pltpu.VMEM((2, 2, 32, n), F32),
        pltpu.VMEM((2, 32, n), F32),
        pltpu.VMEM((2, 2, 32, n), F32),
        pltpu.VMEM((2, LANES, half), BF16),
        pltpu.VMEM((half, 2 * LANES), BF16),
        pltpu.VMEM((2, n, 2 * LANES), F32),
        *[stage] * 8,
        pltpu.VMEM((layers * half, LANES), F32),
        pltpu.VMEM((layers * half, LANES), F32),
        pltpu.VMEM((layers * 2 * layers, wide, LANES), F32),
        pltpu.VMEM((tiles * 32, LANES), F32),
        pltpu.VMEM((tiles * 32, LANES), F32),
        pltpu.VMEM((tiles * 32, LANES), F32),
        pltpu.VMEM((CLASSES, LANES), F32),
        pltpu.VMEM((1, LANES), F32),
        pltpu.VMEM((lat, 1, LANES), F32),
        pltpu.VMEM((1, LANES), F32),
        pltpu.VMEM((freqs, 1, LANES), F32),
        dma((7, tiles)),
        dma((20,)),
        *[dma((ITERS, 2))] * 8,
        dma((1,)),
        dma((layers,)),
        *[dma((1,))] * 8,
    ]
    cell, classes = pl.pallas_call(
        functools.partial(kernel, lat, layers, freqs, n),
        out_shape=(jax.ShapeDtypeStruct((32, n), F32), jax.ShapeDtypeStruct((1, CLASSES), F32)),
        in_specs=[pl.BlockSpec(memory_space=pl.ANY)] * 7,
        out_specs=(pl.BlockSpec(memory_space=pltpu.VMEM), pl.BlockSpec(memory_space=pltpu.VMEM)),
        scratch_shapes=scratch,
        compiler_params=pltpu.CompilerParams(
            collective_id=0, has_side_effects=True, vmem_limit_bytes=55124 * 1024
        ),
    )(
        source.reshape(2, 2, 32, n),
        contrast.reshape(2, 32, n),
        green.reshape(2 * layers, 32, n),
        efield.reshape(2, 2, 32, n),
        cell_class.reshape(32, n),
        jnp.asarray(high),
        jnp.asarray(low),
    )
    return cell.reshape(1, 32, n), classes


def solution(mesh):
    placed = (
        P(None, "freq", None, "layer", "lat", None),
        P(None, "freq", "layer", "lat", None),
        P(None, "freq", None, "layer", "lat", None),
        P(None, "freq", None, "layer", "lat", None),
        P("layer", "lat", None),
    )
    sizes = (mesh.shape["lat"], mesh.shape["layer"], mesh.shape["freq"])
    return jax.shard_map(
        functools.partial(per_device, *sizes),
        mesh=mesh,
        in_specs=placed,
        out_specs=(P("layer", "lat", None), P("layer", None)),
        check_vma=False,
    )
```

```python
import functools
import itertools

import jax
import jax.numpy as jnp
import numpy as np
from jax import lax
from jax.experimental import pallas as pl
from jax.experimental.pallas import tpu as pltpu
from jax.sharding import PartitionSpec as P

ITERS = 2
CLASSES = 8
LANES = 128
MESH = pl.DeviceIdType.MESH
F32 = jnp.float32
BF16 = jnp.bfloat16


def tables(length):
    half = np.arange(length // 2)
    phases = (2 * half[:, None] * half[None, :], half[:, None] * (2 * half[None, :] + 1), (2 * half[:, None] + 1) * half[None, :])
    angles = [(phase % length) * (2.0 * np.pi / length) for phase in phases]
    both = np.stack([np.concatenate([np.cos(angle), np.sin(angle)]) for angle in angles]) / np.sqrt(length)
    high = both.astype(BF16)
    low = (both - high.astype(np.float64)).astype(BF16)
    return high, low


def split(value):
    high = value.astype(BF16)
    return high, (value - high.astype(F32)).astype(BF16)


def dot(a, b):
    return jnp.dot(a, b, preferred_element_type=F32)


def lane_of(shape):
    return lax.broadcasted_iota(jnp.int32, shape, len(shape) - 1)


def turn_lanes(parts):
    parts = list(parts)
    lane = lane_of(parts[0].shape)
    for bit in (1, 2, 4):
        width = 16 * bit
        odd = (lane // width) % 2 == 1
        for q in range(8):
            if q & bit == 0:
                first, second = parts[q], parts[q | bit]
                parts[q] = jnp.where(odd, pltpu.roll(second, width, 1), first)
                parts[q | bit] = jnp.where(odd, second, pltpu.roll(first, LANES - width, 1))
    return parts


def turned(value, sign):
    real = (lane_of(value.shape) // 32) % 2 == 0
    return jnp.where(real, -sign * pltpu.roll(value, LANES - 32, 1), sign * pltpu.roll(value, 32, 1))


def butterfly(value):
    return pltpu.roll(value, 64, 1) + jnp.where(lane_of(value.shape) < 64, value, -value)


def kernel(
    lat, layers, freqs, n,
    src_hbm, con_hbm, grn_hbm, efd_hbm, cls_hbm, high_hbm, low_hbm,
    cell_out, class_out,
    src_raw, con_raw, grn, efd, cls, high, low,
    src, con, field, rows_buf, cols_buf, prod,
    send_a, recv_a, send_b, recv_b, send_c, recv_c, send_d, recv_d,
    send_g, recv_g, wide_g,
    terms, recv_t, cell, lines, part, recv_l, part_f, recv_k,
    load_sem, own_sem,
    sa_sem, ra_sem, sb_sem, rb_sem, sc_sem, rc_sem, sd_sem, rd_sem,
    sg_sem, rg_sem, st_sem, rt_sem, sl_sem, rl_sem, su_sem, ru_sem, sk_sem, rk_sem,
):
    at = {axis: lax.axis_index(axis) for axis in ("lat", "layer", "freq")}
    size = {"lat": lat, "layer": layers, "freq": freqs}

    def others(axis):
        pair = 1 if axis == "freq" else 2
        ring = size[axis] // pair
        found = []
        for k in range(size[axis] - 1):
            i = k // pair
            hop = ring // 2 - (i + 1) // 2 if i % 2 else ring - ring // 2 + i // 2
            peer = lax.rem(at[axis] // pair + hop, ring) * pair
            if pair == 2:
                side = lax.rem(at[axis], 2)
                peer = peer + (1 - side if k % 2 == 0 else side)
            found.append((peer, {axis: peer}))
        return found

    peers = {axis: others(axis) for axis in at}
    half = n // 2
    wide = half // layers

    barrier = pltpu.get_barrier_semaphore()
    for axis in ("lat", "layer", "freq"):
        for _, device in peers[axis]:
            pl.semaphore_signal(barrier, inc=1, device_id=device, device_id_type=MESH)
    tiles = n // LANES

    def by_tile(i, source, target):
        lead = (slice(None),) * (len(source.shape) - 1)
        return [
            pltpu.make_async_copy(source.at[lead + (slice(t * LANES, (t + 1) * LANES),)], target.at[t], load_sem.at[i, t])
            for t in range(tiles)
        ]

    loads = [
        by_tile(0, src_hbm, src_raw),
        by_tile(1, con_hbm, con_raw),
        [pltpu.make_async_copy(high_hbm, high, load_sem.at[2, 0])],
        [pltpu.make_async_copy(low_hbm, low, load_sem.at[3, 0])],
        by_tile(4, grn_hbm, grn),
        by_tile(5, efd_hbm, efd),
        [pltpu.make_async_copy(cls_hbm, cls, load_sem.at[6, 0])],
    ]
    for load in loads:
        for copy in load:
            copy.start()

    def loaded(i):
        for copy in loads[i]:
            copy.wait()

    def remote(device, source, target, send_sem, recv_sem):
        return pltpu.make_async_remote_copy(
            src_ref=source, dst_ref=target, send_sem=send_sem, recv_sem=recv_sem,
            device_id=device, device_id_type=MESH,
        )

    def trade(axis, outgoing, landing, whole, mine, send_sem, recv_sem):
        def everything():
            return remote(peers[axis][0][1], whole[0], whole[1], send_sem, recv_sem)
        def start():
            for peer, device in peers[axis]:
                remote(device, outgoing(peer), landing, send_sem, recv_sem).start()
            if mine is not None:
                mine().start()
        def arrived():
            if peers[axis]:
                everything().wait_recv()
            if mine is not None:
                mine().wait()
        def sent():
            if peers[axis]:
                everything().wait_send()
        return start, arrived, sent

    def swap(axis, source, target, rows, send_sem, recv_sem, own):
        def block(ref, i):
            return ref.at[pl.ds(pl.multiple_of(i * rows, 8), rows)]
        def mine():
            return pltpu.make_async_copy(block(source, at[axis]), block(target, at[axis]), own)
        whole = tuple(ref.at[pl.ds(0, (size[axis] - 1) * rows)] for ref in (source, target))
        return trade(axis, lambda peer: block(source, peer), block(target, at[axis]), whole, mine, send_sem, recv_sem)

    def spread(axis, source, target, send_sem, recv_sem, own):
        def mine():
            return pltpu.make_async_copy(source, target.at[at[axis]], own)
        whole = (target.at[pl.ds(0, size[axis] - 1)],) * 2
        return trade(axis, lambda peer: source, target.at[at[axis]], whole, mine, send_sem, recv_sem)

    def green_block(ref, i):
        return ref.at[pl.ds(pl.multiple_of(i * half, 8), half)]

    def green_copy(device, peer, slot):
        return remote(device, green_block(send_g, peer), green_block(recv_g, slot), sg_sem.at[0], rg_sem.at[slot])

    def exchange(which, step, pol):
        axis, source, target, rows, send_sem, recv_sem = (
            ("lat", send_a, recv_a, 16, sa_sem, ra_sem),
            ("layer", send_b, recv_b, wide, sb_sem, rb_sem),
            ("layer", send_c, recv_c, wide, sc_sem, rc_sem),
            ("lat", send_d, recv_d, 16, sd_sem, rd_sem),
        )[which]
        return swap(
            axis, source.at[step, pol], target.at[step, pol], rows, send_sem.at[step, pol], recv_sem.at[step, pol],
            own_sem.at[(step * 2 + pol) * 4 + which],
        )

    def lane_transform(parity, table):
        whole = rows_buf[parity]
        upper = rows_buf[parity, 0:64]
        out = []
        for base in (0, half):
            product = dot(whole, high[table, base:base + half])
            out.append(product[:64] + product[64:] + dot(upper, low[table, base:base + half]))
        return out

    def row_transform(value, odd_table):
        upper, lower = split(value)
        cols_buf[:, 0:LANES] = upper
        cols_buf[:, LANES:2 * LANES] = lower
        for i, table in enumerate((0, odd_table)):
            prod[i] = dot(high[table], cols_buf[...])
        low_lanes = lane_of((n, LANES)) < 64
        main = jnp.where(low_lanes, prod[0, :, 0:LANES], prod[1, :, 0:LANES])
        main = main + jnp.where(low_lanes, prod[0, :, LANES:2 * LANES], prod[1, :, LANES:2 * LANES])
        tails = [dot(low[table], cols_buf[:, 0:LANES]) for table in (0, odd_table)]
        both = main + jnp.where(low_lanes, tails[0], tails[1])
        return both[:half], both[half:]

    def put_rows(parity, row, lanes, value):
        upper, lower = split(value)
        count = value.shape[0]
        rows_buf[parity, row:row + count, lanes] = upper
        rows_buf[parity, 64 + row:64 + row + count, lanes] = lower

    def forward_lanes(step, pol):
        for piece, value in enumerate(
            (
                con[0] * field[0, pol] - con[1] * field[1, pol],
                con[0] * field[1, pol] + con[1] * field[0, pol],
            )
        ):
            put_rows(0, piece * 32, slice(None), value[:, :half] + value[:, half:])
            put_rows(1, piece * 32, slice(None), value[:, :half] - value[:, half:])
        pieces = []
        for parity in range(2):
            cosine, sine = lane_transform(parity, parity)
            pieces.append((cosine[:32] + sine[32:], cosine[32:] - sine[:32]))
        for tile in range(half // LANES):
            lanes = slice(tile * LANES, (tile + 1) * LANES)
            blocks = turn_lanes(
                [pieces[q % 2][q // 2 % 2][q // 4 * 16:q // 4 * 16 + 16, lanes] for q in range(8)]
            )
            for g, block in enumerate(blocks):
                row = (tile * 8 + g) * 16
                send_a[step, pol, row:row + 16] = block

    def inverse_lanes(step, pol):
        for tile in range(half // LANES):
            lanes = slice(tile * LANES, (tile + 1) * LANES)
            blocks = turn_lanes([recv_d[step, pol, pl.ds((tile * 8 + g) * 16, 16)] for g in range(8)])
            for q, block in enumerate(blocks):
                put_rows(q % 2, q // 2 % 2 * 32 + q // 4 * 16, lanes, block)
        pieces = []
        for parity in range(2):
            cosine, sine = lane_transform(parity, 2 * parity)
            pieces.append((cosine[:32] - sine[32:], cosine[32:] + sine[:32]))
        for lanes, sign in ((slice(0, half), 1.0), (slice(half, n), -1.0)):
            real, imag = (pieces[0][i] + sign * pieces[1][i] for i in range(2))
            field[0, pol, :, lanes] = src[0, pol, :, lanes] + con[0, :, lanes] * real - con[1, :, lanes] * imag
            field[1, pol, :, lanes] = src[1, pol, :, lanes] + con[0, :, lanes] * imag + con[1, :, lanes] * real

    def prepare_green():
        loaded(4)
        for pair in range(layers):
            for tile in range(half // LANES):
                rows = [
                    grn[end * (half // LANES) + tile, 2 * pair + s, pl.ds(parity, 16, stride=2)]
                    for end in range(2) for s in range(2) for parity in range(2)
                ]
                flipped = jnp.concatenate(rows, axis=0).T
                for part_of in range(LANES // wide):
                    row = ((tile * LANES // wide + part_of) * layers + pair) * wide
                    send_g[row:row + wide] = flipped[part_of * wide:(part_of + 1) * wide]

    def widen(source, l):
        for pair in range(layers):
            value = source[pl.ds(pl.multiple_of((l * layers + pair) * wide, 8), wide)]
            odd = (lane_of(value.shape) // 32) % 2 == 1
            spot = (l * layers + pair) * 2
            wide_g[spot] = jnp.where(odd, pltpu.roll(value, 32, 1), value)
            wide_g[spot + 1] = jnp.where(odd, value, pltpu.roll(value, LANES - 32, 1))

    def mix(step, pol):
        def rows(r, carry):
            base = pl.multiple_of(r * 8, 8)
            sums = [None] * layers
            for l in range(layers):
                value = recv_b[step, pol, pl.ds(pl.multiple_of(l * wide + base, 8), 8)]
                side = turned(value, 1.0)
                for o in range(layers):
                    term = (
                        wide_g[l * 2 * layers + o, pl.ds(base, 8)] * value
                        + wide_g[l * 2 * layers + layers + o, pl.ds(base, 8)] * side
                    )
                    sums[o] = term if l == 0 else sums[o] + term
            for o in range(layers):
                send_c[step, pol, pl.ds(pl.multiple_of(o * wide + base, 8), 8)] = sums[o]
            return carry

        lax.fori_loop(0, wide // 8, rows, 0, unroll=2)

    even_odd = [(slice(parity * 16, parity * 16 + 16), pl.ds(parity, 16, stride=2)) for parity in range(2)]
    loaded(1)
    for mine, stride in even_odd:
        for piece, t in itertools.product(range(2), range(tiles)):
            con[piece, mine, t * LANES:(t + 1) * LANES] = con_raw[t, piece, stride]
    loaded(0)
    for mine, stride in even_odd:
        for piece, pol, t in itertools.product(range(2), range(2), range(tiles)):
            value = src_raw[t, piece, pol, stride]
            src[piece, pol, mine, t * LANES:(t + 1) * LANES] = value
            field[piece, pol, mine, t * LANES:(t + 1) * LANES] = value
    loaded(2)
    loaded(3)

    def iterate(step, carry):
        for pol in range(2):
            @pl.when(step > 0)
            def _():
                exchange(3, step - 1, pol)[1]()
                inverse_lanes(step - 1, pol)

            forward_lanes(step, pol)

            if pol == 0:
                @pl.when(step == 0)
                def _():
                    prepare_green()
                    pl.semaphore_wait(barrier, lat + layers + freqs - 3)

            exchange(0, step, pol)[0]()

            if pol == 0:
                @pl.when(step == 0)
                def _():
                    for peer, device in peers["layer"]:
                        green_copy(device, peer, at["layer"]).start()

        for pol in range(2):
            exchange(0, step, pol)[1]()
            cosine, sine = row_transform(recv_a[step, pol], 1)
            send_b[step, pol] = butterfly(cosine + turned(sine, -1.0))
            exchange(1, step, pol)[0]()

        @pl.when(step == 0)
        def _():
            widen(send_g, at["layer"])
            for peer, device in peers["layer"]:
                green_copy(device, peer, peer).wait_recv()
                widen(recv_g, peer)

        for pol in range(2):
            exchange(1, step, pol)[1]()
            mix(step, pol)
            exchange(2, step, pol)[0]()

        for pol in range(2):
            exchange(2, step, pol)[1]()
            cosine, sine = row_transform(butterfly(recv_c[step, pol]), 2)
            send_d[step, pol] = cosine + turned(sine, 1.0)
            exchange(3, step, pol)[0]()
        return carry

    lax.fori_loop(0, ITERS, iterate, 0)

    loaded(5)
    loaded(6)
    for pol in range(2):
        exchange(3, ITERS - 1, pol)[1]()
        inverse_lanes(ITERS - 1, pol)
        for parity, t in itertools.product(range(2), range(tiles)):
            mine = slice(parity * 16, parity * 16 + 16)
            lanes = slice(t * LANES, (t + 1) * LANES)
            stride = pl.ds(parity, 16, stride=2)
            value = efd[t, 0, pol, stride] * field[0, pol, mine, lanes] - efd[t, 1, pol, stride] * field[1, pol, mine, lanes]
            spots = pl.ds(t * 32 + parity, 16, stride=2)
            terms[spots] = value if pol == 0 else terms[spots] + value
    own_rows = tiles * 32 // freqs
    scatter = swap("freq", terms, recv_t, own_rows, st_sem.at[0], rt_sem.at[0], own_sem.at[17])
    scatter[0]()

    for c in range(CLASSES):
        kept = [
            jnp.where(cls[:, t * LANES:(t + 1) * LANES] == c, terms[t * 32:(t + 1) * 32], 0.0) for t in range(tiles)
        ]
        lines[c:c + 1] = jnp.sum(sum(kept), axis=0, keepdims=True)
    sums = jnp.sum(lines[...], axis=1, keepdims=True)
    spot = lax.broadcasted_iota(jnp.int32, (CLASSES, LANES), 0) == lane_of((CLASSES, LANES))
    part[...] = jnp.sum(jnp.where(spot, sums, 0.0), axis=0, keepdims=True)
    lat_sums = spread("lat", part, recv_l, sl_sem.at[0], rl_sem.at[0], own_sem.at[18])
    lat_sums[0]()

    scatter[1]()
    mine = recv_t[0:own_rows]
    for f in range(1, freqs):
        mine = mine + recv_t[f * own_rows:(f + 1) * own_rows]
    own = pl.ds(pl.multiple_of(at["freq"] * own_rows, 8), own_rows)
    cell[own] = mine

    spots = tuple(cell.at[pl.ds(0, (freqs - 1) * own_rows)] for _ in range(2))
    gather = trade("freq", lambda peer: cell.at[own], cell.at[own], spots, None, su_sem.at[0], ru_sem.at[0])
    gather[0]()

    lat_sums[1]()
    part_f[...] = jnp.sum(recv_l[...], axis=0)
    freq_sums = spread("freq", part_f, recv_k, sk_sem.at[0], rk_sem.at[0], own_sem.at[19])
    freq_sums[0]()

    gather[1]()
    for t in range(tiles):
        cell_out[:, t * LANES:(t + 1) * LANES] = cell[t * 32:(t + 1) * 32]
    freq_sums[1]()
    class_out[...] = (jnp.sum(recv_k[...], axis=0) / float(n))[:, :CLASSES]

    def drain(step, carry):
        for pol in range(2):
            for which in range(4):
                exchange(which, step, pol)[2]()
        return carry

    lax.fori_loop(0, ITERS, drain, 0)
    for peer, device in peers["layer"]:
        green_copy(device, peer, at["layer"]).wait_send()
    scatter[2]()
    lat_sums[2]()
    gather[2]()
    freq_sums[2]()


def per_device(lat, layers, freqs, source, contrast, green, efield, cell_class):
    n = source.shape[5]
    high, low = tables(n)
    half = n // 2
    wide = half // layers
    dma = pltpu.SemaphoreType.DMA
    stage = pltpu.VMEM((ITERS, 2, half, LANES), F32)
    tiles = n // LANES
    scratch = [
        pltpu.VMEM((tiles, 2, 2, 32, LANES), F32),
        pltpu.VMEM((tiles, 2, 32, LANES), F32),
        pltpu.VMEM((tiles, 2 * layers, 32, LANES), F32),
        pltpu.VMEM((tiles, 2, 2, 32, LANES), F32),
        pltpu.VMEM((32, n), jnp.int32),
        pltpu.VMEM((3, n, half), BF16),
        pltpu.VMEM((3, n, half), BF16),
        pltpu.VMEM((2, 2, 32, n), F32),
        pltpu.VMEM((2, 32, n), F32),
        pltpu.VMEM((2, 2, 32, n), F32),
        pltpu.VMEM((2, LANES, half), BF16),
        pltpu.VMEM((half, 2 * LANES), BF16),
        pltpu.VMEM((2, n, 2 * LANES), F32),
        *[stage] * 8,
        pltpu.VMEM((layers * half, LANES), F32),
        pltpu.VMEM((layers * half, LANES), F32),
        pltpu.VMEM((layers * 2 * layers, wide, LANES), F32),
        pltpu.VMEM((tiles * 32, LANES), F32),
        pltpu.VMEM((tiles * 32, LANES), F32),
        pltpu.VMEM((tiles * 32, LANES), F32),
        pltpu.VMEM((CLASSES, LANES), F32),
        pltpu.VMEM((1, LANES), F32),
        pltpu.VMEM((lat, 1, LANES), F32),
        pltpu.VMEM((1, LANES), F32),
        pltpu.VMEM((freqs, 1, LANES), F32),
        dma((7, tiles)),
        dma((20,)),
        *[dma((ITERS, 2))] * 8,
        dma((1,)),
        dma((layers,)),
        *[dma((1,))] * 8,
    ]
    cell, classes = pl.pallas_call(
        functools.partial(kernel, lat, layers, freqs, n),
        out_shape=(jax.ShapeDtypeStruct((32, n), F32), jax.ShapeDtypeStruct((1, CLASSES), F32)),
        in_specs=[pl.BlockSpec(memory_space=pl.ANY)] * 7,
        out_specs=(pl.BlockSpec(memory_space=pltpu.VMEM), pl.BlockSpec(memory_space=pltpu.VMEM)),
        scratch_shapes=scratch,
        compiler_params=pltpu.CompilerParams(
            collective_id=0, has_side_effects=True, vmem_limit_bytes=55124 * 1024
        ),
    )(
        source.reshape(2, 2, 32, n),
        contrast.reshape(2, 32, n),
        green.reshape(2 * layers, 32, n),
        efield.reshape(2, 2, 32, n),
        cell_class.reshape(32, n),
        jnp.asarray(high),
        jnp.asarray(low),
    )
    return cell.reshape(1, 32, n), classes


def solution(mesh):
    placed = (
        P(None, "freq", None, "layer", "lat", None),
        P(None, "freq", "layer", "lat", None),
        P(None, "freq", None, "layer", "lat", None),
        P(None, "freq", None, "layer", "lat", None),
        P("layer", "lat", None),
    )
    sizes = (mesh.shape["lat"], mesh.shape["layer"], mesh.shape["freq"])
    return jax.shard_map(
        functools.partial(per_device, *sizes),
        mesh=mesh,
        in_specs=placed,
        out_specs=(P("layer", "lat", None), P("layer", None)),
        check_vma=False,
    )
```

```python
import functools
import itertools

import jax
import jax.numpy as jnp
import numpy as np
from jax import lax
from jax.experimental import pallas as pl
from jax.experimental.pallas import tpu as pltpu
from jax.sharding import PartitionSpec as P

ITERS = 2
CLASSES = 8
LANES = 128
MESH = pl.DeviceIdType.MESH
F32 = jnp.float32
BF16 = jnp.bfloat16


def tables(length):
    half = np.arange(length // 2)
    phases = (2 * half[:, None] * half[None, :], half[:, None] * (2 * half[None, :] + 1), (2 * half[:, None] + 1) * half[None, :])
    angles = [(phase % length) * (2.0 * np.pi / length) for phase in phases]
    both = np.stack([np.concatenate([np.cos(angle), np.sin(angle)]) for angle in angles]) / np.sqrt(length)
    high = both.astype(BF16)
    low = (both - high.astype(np.float64)).astype(BF16)
    return high, low


def split(value):
    high = value.astype(BF16)
    return high, (value - high.astype(F32)).astype(BF16)


def dot(a, b):
    return jnp.dot(a, b, preferred_element_type=F32)


def lane_of(shape):
    return lax.broadcasted_iota(jnp.int32, shape, len(shape) - 1)


def turn_lanes(parts):
    parts = list(parts)
    lane = lane_of(parts[0].shape)
    for bit in (1, 2, 4):
        width = 16 * bit
        odd = (lane // width) % 2 == 1
        for q in range(8):
            if q & bit == 0:
                first, second = parts[q], parts[q | bit]
                parts[q] = jnp.where(odd, pltpu.roll(second, width, 1), first)
                parts[q | bit] = jnp.where(odd, second, pltpu.roll(first, LANES - width, 1))
    return parts


def turned(value, sign):
    real = (lane_of(value.shape) // 32) % 2 == 0
    return jnp.where(real, -sign * pltpu.roll(value, LANES - 32, 1), sign * pltpu.roll(value, 32, 1))


def butterfly(value):
    return pltpu.roll(value, 64, 1) + jnp.where(lane_of(value.shape) < 64, value, -value)


def kernel(
    lat, layers, freqs, n,
    src_hbm, con_hbm, grn_hbm, efd_hbm, cls_hbm, high_hbm, low_hbm,
    cell_out, class_out,
    src_raw, con_raw, grn, efd, cls, high, low,
    src, con, field, rows_buf, cols_buf, prod,
    send_a, recv_a, send_b, recv_b, send_c, recv_c, send_d, recv_d,
    send_g, recv_g, wide_g,
    terms, recv_t, cell, lines, part, recv_l, part_f, recv_k,
    load_sem, own_sem,
    sa_sem, ra_sem, sb_sem, rb_sem, sc_sem, rc_sem, sd_sem, rd_sem,
    sg_sem, rg_sem, st_sem, rt_sem, sl_sem, rl_sem, su_sem, ru_sem, sk_sem, rk_sem,
):
    at = {axis: lax.axis_index(axis) for axis in ("lat", "layer", "freq")}
    size = {"lat": lat, "layer": layers, "freq": freqs}

    def others(axis):
        pair = 1 if axis == "freq" else 2
        ring = size[axis] // pair
        spots = [(hop, flip) for hop in range(ring) for flip in range(pair) if hop or flip]
        across = 1 if axis == "layer" else 0
        spots.sort(key=lambda spot: (-min(spot[0], ring - spot[0]) - across * spot[1], -spot[1] * across, spot[1], spot[0]))
        found = []
        for hop, flip in spots:
            peer = lax.rem(at[axis] // pair + hop, ring) * pair
            if pair == 2:
                side = lax.rem(at[axis], 2)
                peer = peer + (1 - side if flip else side)
            found.append((peer, {axis: peer}))
        return found

    peers = {axis: others(axis) for axis in at}
    half = n // 2
    wide = half // layers

    barrier = pltpu.get_barrier_semaphore()
    for axis in ("lat", "layer", "freq"):
        for _, device in peers[axis]:
            pl.semaphore_signal(barrier, inc=1, device_id=device, device_id_type=MESH)
    tiles = n // LANES

    def by_tile(i, source, target):
        lead = (slice(None),) * (len(source.shape) - 1)
        return [
            pltpu.make_async_copy(source.at[lead + (slice(t * LANES, (t + 1) * LANES),)], target.at[t], load_sem.at[i, t])
            for t in range(tiles)
        ]

    loads = [
        by_tile(0, src_hbm, src_raw),
        by_tile(1, con_hbm, con_raw),
        [pltpu.make_async_copy(high_hbm, high, load_sem.at[2, 0])],
        [pltpu.make_async_copy(low_hbm, low, load_sem.at[3, 0])],
        by_tile(4, grn_hbm, grn),
        by_tile(5, efd_hbm, efd),
        [pltpu.make_async_copy(cls_hbm, cls, load_sem.at[6, 0])],
    ]
    for load in loads:
        for copy in load:
            copy.start()

    def loaded(i):
        for copy in loads[i]:
            copy.wait()

    def remote(device, source, target, send_sem, recv_sem):
        return pltpu.make_async_remote_copy(
            src_ref=source, dst_ref=target, send_sem=send_sem, recv_sem=recv_sem,
            device_id=device, device_id_type=MESH,
        )

    def trade(axis, outgoing, landing, whole, mine, send_sem, recv_sem):
        def everything():
            return remote(peers[axis][0][1], whole[0], whole[1], send_sem, recv_sem)
        def start():
            for peer, device in peers[axis]:
                remote(device, outgoing(peer), landing, send_sem, recv_sem).start()
            if mine is not None:
                mine().start()
        def arrived():
            if peers[axis]:
                everything().wait_recv()
            if mine is not None:
                mine().wait()
        def sent():
            if peers[axis]:
                everything().wait_send()
        return start, arrived, sent

    def swap(axis, source, target, rows, send_sem, recv_sem, own):
        def block(ref, i):
            return ref.at[pl.ds(pl.multiple_of(i * rows, 8), rows)]
        def mine():
            return pltpu.make_async_copy(block(source, at[axis]), block(target, at[axis]), own)
        whole = tuple(ref.at[pl.ds(0, (size[axis] - 1) * rows)] for ref in (source, target))
        return trade(axis, lambda peer: block(source, peer), block(target, at[axis]), whole, mine, send_sem, recv_sem)

    def spread(axis, source, target, send_sem, recv_sem, own):
        def mine():
            return pltpu.make_async_copy(source, target.at[at[axis]], own)
        whole = (target.at[pl.ds(0, size[axis] - 1)],) * 2
        return trade(axis, lambda peer: source, target.at[at[axis]], whole, mine, send_sem, recv_sem)

    def green_block(ref, i):
        return ref.at[pl.ds(pl.multiple_of(i * half, 8), half)]

    def green_copy(device, peer, slot):
        return remote(device, green_block(send_g, peer), green_block(recv_g, slot), sg_sem.at[0], rg_sem.at[slot])

    def exchange(which, step, pol):
        axis, source, target, rows, send_sem, recv_sem = (
            ("lat", send_a, recv_a, 16, sa_sem, ra_sem),
            ("layer", send_b, recv_b, wide, sb_sem, rb_sem),
            ("layer", send_c, recv_c, wide, sc_sem, rc_sem),
            ("lat", send_d, recv_d, 16, sd_sem, rd_sem),
        )[which]
        return swap(
            axis, source.at[step, pol], target.at[step, pol], rows, send_sem.at[step, pol], recv_sem.at[step, pol],
            own_sem.at[(step * 2 + pol) * 4 + which],
        )

    def lane_transform(parity, table):
        whole = rows_buf[parity]
        upper = rows_buf[parity, 0:64]
        out = []
        for base in (0, half):
            product = dot(whole, high[table, base:base + half])
            out.append(product[:64] + product[64:] + dot(upper, low[table, base:base + half]))
        return out

    def row_transform(value, odd_table):
        upper, lower = split(value)
        cols_buf[:, 0:LANES] = upper
        cols_buf[:, LANES:2 * LANES] = lower
        for i, table in enumerate((0, odd_table)):
            prod[i] = dot(high[table], cols_buf[...])
        low_lanes = lane_of((n, LANES)) < 64
        main = jnp.where(low_lanes, prod[0, :, 0:LANES], prod[1, :, 0:LANES])
        main = main + jnp.where(low_lanes, prod[0, :, LANES:2 * LANES], prod[1, :, LANES:2 * LANES])
        tails = [dot(low[table], cols_buf[:, 0:LANES]) for table in (0, odd_table)]
        both = main + jnp.where(low_lanes, tails[0], tails[1])
        return both[:half], both[half:]

    def put_rows(parity, row, lanes, value):
        upper, lower = split(value)
        count = value.shape[0]
        rows_buf[parity, row:row + count, lanes] = upper
        rows_buf[parity, 64 + row:64 + row + count, lanes] = lower

    def forward_lanes(step, pol):
        for piece, value in enumerate(
            (
                con[0] * field[0, pol] - con[1] * field[1, pol],
                con[0] * field[1, pol] + con[1] * field[0, pol],
            )
        ):
            put_rows(0, piece * 32, slice(None), value[:, :half] + value[:, half:])
            put_rows(1, piece * 32, slice(None), value[:, :half] - value[:, half:])
        pieces = []
        for parity in range(2):
            cosine, sine = lane_transform(parity, parity)
            pieces.append((cosine[:32] + sine[32:], cosine[32:] - sine[:32]))
        for tile in range(half // LANES):
            lanes = slice(tile * LANES, (tile + 1) * LANES)
            blocks = turn_lanes(
                [pieces[q % 2][q // 2 % 2][q // 4 * 16:q // 4 * 16 + 16, lanes] for q in range(8)]
            )
            for g, block in enumerate(blocks):
                row = (tile * 8 + g) * 16
                send_a[step, pol, row:row + 16] = block

    def inverse_lanes(step, pol):
        for tile in range(half // LANES):
            lanes = slice(tile * LANES, (tile + 1) * LANES)
            blocks = turn_lanes([recv_d[step, pol, pl.ds((tile * 8 + g) * 16, 16)] for g in range(8)])
            for q, block in enumerate(blocks):
                put_rows(q % 2, q // 2 % 2 * 32 + q // 4 * 16, lanes, block)
        pieces = []
        for parity in range(2):
            cosine, sine = lane_transform(parity, 2 * parity)
            pieces.append((cosine[:32] - sine[32:], cosine[32:] + sine[:32]))
        for lanes, sign in ((slice(0, half), 1.0), (slice(half, n), -1.0)):
            real, imag = (pieces[0][i] + sign * pieces[1][i] for i in range(2))
            field[0, pol, :, lanes] = src[0, pol, :, lanes] + con[0, :, lanes] * real - con[1, :, lanes] * imag
            field[1, pol, :, lanes] = src[1, pol, :, lanes] + con[0, :, lanes] * imag + con[1, :, lanes] * real

    def prepare_green():
        loaded(4)
        for pair in range(layers):
            for tile in range(half // LANES):
                rows = [
                    grn[end * (half // LANES) + tile, 2 * pair + s, pl.ds(parity, 16, stride=2)]
                    for end in range(2) for s in range(2) for parity in range(2)
                ]
                flipped = jnp.concatenate(rows, axis=0).T
                for part_of in range(LANES // wide):
                    row = ((tile * LANES // wide + part_of) * layers + pair) * wide
                    send_g[row:row + wide] = flipped[part_of * wide:(part_of + 1) * wide]

    def widen(source, l):
        for pair in range(layers):
            value = source[pl.ds(pl.multiple_of((l * layers + pair) * wide, 8), wide)]
            odd = (lane_of(value.shape) // 32) % 2 == 1
            spot = (l * layers + pair) * 2
            wide_g[spot] = jnp.where(odd, pltpu.roll(value, 32, 1), value)
            wide_g[spot + 1] = jnp.where(odd, value, pltpu.roll(value, LANES - 32, 1))

    def mix(step, pol):
        def rows(r, carry):
            base = pl.multiple_of(r * 8, 8)
            sums = [None] * layers
            for l in range(layers):
                value = recv_b[step, pol, pl.ds(pl.multiple_of(l * wide + base, 8), 8)]
                side = turned(value, 1.0)
                for o in range(layers):
                    term = (
                        wide_g[l * 2 * layers + o, pl.ds(base, 8)] * value
                        + wide_g[l * 2 * layers + layers + o, pl.ds(base, 8)] * side
                    )
                    sums[o] = term if l == 0 else sums[o] + term
            for o in range(layers):
                send_c[step, pol, pl.ds(pl.multiple_of(o * wide + base, 8), 8)] = sums[o]
            return carry

        lax.fori_loop(0, wide // 8, rows, 0, unroll=2)

    even_odd = [(slice(parity * 16, parity * 16 + 16), pl.ds(parity, 16, stride=2)) for parity in range(2)]
    loaded(1)
    for mine, stride in even_odd:
        for piece, t in itertools.product(range(2), range(tiles)):
            con[piece, mine, t * LANES:(t + 1) * LANES] = con_raw[t, piece, stride]
    loaded(0)
    for mine, stride in even_odd:
        for piece, pol, t in itertools.product(range(2), range(2), range(tiles)):
            value = src_raw[t, piece, pol, stride]
            src[piece, pol, mine, t * LANES:(t + 1) * LANES] = value
            field[piece, pol, mine, t * LANES:(t + 1) * LANES] = value
    loaded(2)
    loaded(3)

    def iterate(step, carry):
        for pol in range(2):
            @pl.when(step > 0)
            def _():
                exchange(3, step - 1, pol)[1]()
                inverse_lanes(step - 1, pol)

            forward_lanes(step, pol)

            if pol == 0:
                @pl.when(step == 0)
                def _():
                    prepare_green()
                    pl.semaphore_wait(barrier, lat + layers + freqs - 3)

            exchange(0, step, pol)[0]()

            if pol == 0:
                @pl.when(step == 0)
                def _():
                    for peer, device in peers["layer"]:
                        green_copy(device, peer, at["layer"]).start()

        for pol in range(2):
            exchange(0, step, pol)[1]()
            cosine, sine = row_transform(recv_a[step, pol], 1)
            send_b[step, pol] = butterfly(cosine + turned(sine, -1.0))
            exchange(1, step, pol)[0]()

        @pl.when(step == 0)
        def _():
            widen(send_g, at["layer"])
            for peer, device in peers["layer"]:
                green_copy(device, peer, peer).wait_recv()
                widen(recv_g, peer)

        for pol in range(2):
            exchange(1, step, pol)[1]()
            mix(step, pol)
            exchange(2, step, pol)[0]()

        for pol in range(2):
            exchange(2, step, pol)[1]()
            cosine, sine = row_transform(butterfly(recv_c[step, pol]), 2)
            send_d[step, pol] = cosine + turned(sine, 1.0)
            exchange(3, step, pol)[0]()
        return carry

    lax.fori_loop(0, ITERS, iterate, 0)

    loaded(5)
    loaded(6)
    for pol in range(2):
        exchange(3, ITERS - 1, pol)[1]()
        inverse_lanes(ITERS - 1, pol)
        for parity, t in itertools.product(range(2), range(tiles)):
            mine = slice(parity * 16, parity * 16 + 16)
            lanes = slice(t * LANES, (t + 1) * LANES)
            stride = pl.ds(parity, 16, stride=2)
            value = efd[t, 0, pol, stride] * field[0, pol, mine, lanes] - efd[t, 1, pol, stride] * field[1, pol, mine, lanes]
            spots = pl.ds(t * 32 + parity, 16, stride=2)
            terms[spots] = value if pol == 0 else terms[spots] + value
    own_rows = tiles * 32 // freqs
    scatter = swap("freq", terms, recv_t, own_rows, st_sem.at[0], rt_sem.at[0], own_sem.at[17])
    scatter[0]()

    for c in range(CLASSES):
        kept = [
            jnp.where(cls[:, t * LANES:(t + 1) * LANES] == c, terms[t * 32:(t + 1) * 32], 0.0) for t in range(tiles)
        ]
        lines[c:c + 1] = jnp.sum(sum(kept), axis=0, keepdims=True)
    sums = jnp.sum(lines[...], axis=1, keepdims=True)
    spot = lax.broadcasted_iota(jnp.int32, (CLASSES, LANES), 0) == lane_of((CLASSES, LANES))
    part[...] = jnp.sum(jnp.where(spot, sums, 0.0), axis=0, keepdims=True)
    lat_sums = spread("lat", part, recv_l, sl_sem.at[0], rl_sem.at[0], own_sem.at[18])
    lat_sums[0]()

    scatter[1]()
    mine = recv_t[0:own_rows]
    for f in range(1, freqs):
        mine = mine + recv_t[f * own_rows:(f + 1) * own_rows]
    own = pl.ds(pl.multiple_of(at["freq"] * own_rows, 8), own_rows)
    cell[own] = mine

    spots = tuple(cell.at[pl.ds(0, (freqs - 1) * own_rows)] for _ in range(2))
    gather = trade("freq", lambda peer: cell.at[own], cell.at[own], spots, None, su_sem.at[0], ru_sem.at[0])
    gather[0]()

    lat_sums[1]()
    part_f[...] = jnp.sum(recv_l[...], axis=0)
    freq_sums = spread("freq", part_f, recv_k, sk_sem.at[0], rk_sem.at[0], own_sem.at[19])
    freq_sums[0]()

    gather[1]()
    for t in range(tiles):
        cell_out[:, t * LANES:(t + 1) * LANES] = cell[t * 32:(t + 1) * 32]
    freq_sums[1]()
    class_out[...] = (jnp.sum(recv_k[...], axis=0) / float(n))[:, :CLASSES]

    def drain(step, carry):
        for pol in range(2):
            for which in range(4):
                exchange(which, step, pol)[2]()
        return carry

    lax.fori_loop(0, ITERS, drain, 0)
    for peer, device in peers["layer"]:
        green_copy(device, peer, at["layer"]).wait_send()
    scatter[2]()
    lat_sums[2]()
    gather[2]()
    freq_sums[2]()


def per_device(lat, layers, freqs, source, contrast, green, efield, cell_class):
    n = source.shape[5]
    high, low = tables(n)
    half = n // 2
    wide = half // layers
    dma = pltpu.SemaphoreType.DMA
    stage = pltpu.VMEM((ITERS, 2, half, LANES), F32)
    tiles = n // LANES
    scratch = [
        pltpu.VMEM((tiles, 2, 2, 32, LANES), F32),
        pltpu.VMEM((tiles, 2, 32, LANES), F32),
        pltpu.VMEM((tiles, 2 * layers, 32, LANES), F32),
        pltpu.VMEM((tiles, 2, 2, 32, LANES), F32),
        pltpu.VMEM((32, n), jnp.int32),
        pltpu.VMEM((3, n, half), BF16),
        pltpu.VMEM((3, n, half), BF16),
        pltpu.VMEM((2, 2, 32, n), F32),
        pltpu.VMEM((2, 32, n), F32),
        pltpu.VMEM((2, 2, 32, n), F32),
        pltpu.VMEM((2, LANES, half), BF16),
        pltpu.VMEM((half, 2 * LANES), BF16),
        pltpu.VMEM((2, n, 2 * LANES), F32),
        *[stage] * 8,
        pltpu.VMEM((layers * half, LANES), F32),
        pltpu.VMEM((layers * half, LANES), F32),
        pltpu.VMEM((layers * 2 * layers, wide, LANES), F32),
        pltpu.VMEM((tiles * 32, LANES), F32),
        pltpu.VMEM((tiles * 32, LANES), F32),
        pltpu.VMEM((tiles * 32, LANES), F32),
        pltpu.VMEM((CLASSES, LANES), F32),
        pltpu.VMEM((1, LANES), F32),
        pltpu.VMEM((lat, 1, LANES), F32),
        pltpu.VMEM((1, LANES), F32),
        pltpu.VMEM((freqs, 1, LANES), F32),
        dma((7, tiles)),
        dma((20,)),
        *[dma((ITERS, 2))] * 8,
        dma((1,)),
        dma((layers,)),
        *[dma((1,))] * 8,
    ]
    cell, classes = pl.pallas_call(
        functools.partial(kernel, lat, layers, freqs, n),
        out_shape=(jax.ShapeDtypeStruct((32, n), F32), jax.ShapeDtypeStruct((1, CLASSES), F32)),
        in_specs=[pl.BlockSpec(memory_space=pl.ANY)] * 7,
        out_specs=(pl.BlockSpec(memory_space=pltpu.VMEM), pl.BlockSpec(memory_space=pltpu.VMEM)),
        scratch_shapes=scratch,
        compiler_params=pltpu.CompilerParams(
            collective_id=0, has_side_effects=True, vmem_limit_bytes=55124 * 1024
        ),
    )(
        source.reshape(2, 2, 32, n),
        contrast.reshape(2, 32, n),
        green.reshape(2 * layers, 32, n),
        efield.reshape(2, 2, 32, n),
        cell_class.reshape(32, n),
        jnp.asarray(high),
        jnp.asarray(low),
    )
    return cell.reshape(1, 32, n), classes


def solution(mesh):
    placed = (
        P(None, "freq", None, "layer", "lat", None),
        P(None, "freq", "layer", "lat", None),
        P(None, "freq", None, "layer", "lat", None),
        P(None, "freq", None, "layer", "lat", None),
        P("layer", "lat", None),
    )
    sizes = (mesh.shape["lat"], mesh.shape["layer"], mesh.shape["freq"])
    return jax.shard_map(
        functools.partial(per_device, *sizes),
        mesh=mesh,
        in_specs=placed,
        out_specs=(P("layer", "lat", None), P("layer", None)),
        check_vma=False,
    )
```
